32 devices in a mesh: stn: 4 (over y, core), chan: 8 (over z, x).
Axes of the slice: x: 2, y: 2, z: 4, core: 2. Of those that a mesh axis runs over, the one named last changes fastest.
Arguments:
- voltages: bfloat16 [1024, 27, 2, 4096], P(('stn', 'chan')), may hold values from -6 to 6
- filter_taps: float32 [12, 4096], replicated, may hold values from -1.75 to 1.75
- beam_stations: int32 [16, 128], replicated, may hold values from 0 to 511, all different within a row
- beam_gain: float32 [16, 128], P('stn'), may hold values from 0.25 to 4
- beam_delay: float32 [16, 128], P('stn'), may hold values from -8 to 8
- block_pairs: int32 [16, 2], replicated, may hold values from 0 to 15, as said below
Outputs:
- visibilities: bfloat16 [1024, 16, 64, 128], P(('stn', 'chan'))
- beam_spectra: bfloat16 [16, 2, 4096, 32], P(None, None, ('stn', 'chan'))
The draws below stay inside these ranges and needn't reach their ends.
Inputs may be any that keep to these rules, and one draw needn't show every extreme that they name: `beam_stations`: each row names 128 different stations, and every station is named by some row. `block_pairs`: rows come in 2 rounds of 8 rows; within a round every block appears exactly once; the two entries of a row differ, and no two rows name the same two blocks.
All inputs are finite; a program needn't handle non-finite values.
Results may differ from the reference program's by a relative error of at most 0.0058.
Values may be sent and summed in bfloat16 or wider, within the bound.
A program may use at most 192 MiB of HBM per device.

```python
import math
from functools import partial
import jax
import jax.numpy as jnp
import numpy as np
from jax import lax

STATIONS = 512
NFFT = 4096
BEAMS = 16
TAPS = 12
FAVG = 4
BLK = 64
LIST = 128
SPEC = 16
ROUNDS = 2
INPUTS = 1024
FRAMES = 27
NBLK = 16
OUTCH = 1024


def draw_voltages(key, part):
    key_noise = jax.random.fold_in(key, 11)
    key_common = jax.random.fold_in(key, 12)
    key_phase = jax.random.fold_in(key, 13)
    noise = jax.random.normal(key_noise, (INPUTS, FRAMES, 2, NFFT), jnp.float32)
    common = jax.random.normal(key_common, (1, FRAMES, 2, NFFT), jnp.float32)
    phases = jax.random.uniform(key_phase, (INPUTS, 1, 1, 1), jnp.float32, -math.pi, math.pi)
    cosine = jnp.cos(phases)
    sine_part = jnp.sin(phases)
    common_real = common[:, :, 0:1, :]
    common_imag = common[:, :, 1:2, :]
    rotated = jnp.concatenate([cosine * common_real - sine_part * common_imag, sine_part * common_real + cosine * common_imag], axis=2)
    values = (noise + rotated) * 0.70710677
    return jnp.clip(values, -6.0, 6.0).astype(jnp.bfloat16)


def draw_block_pairs(key, part):
    per_round = NBLK // 2
    pair_list = []
    for round_index in range(ROUNDS):
        pair_list.append((round_index, NBLK - 1))
        for step_index in range(1, per_round):
            pair_list.append(((round_index + step_index) % (NBLK - 1), (round_index - step_index) % (NBLK - 1)))
    roster = jnp.asarray(np.array(pair_list, dtype=np.int32))
    relabel = jax.random.permutation(jax.random.fold_in(key, 21), NBLK).astype(jnp.int32)
    labelled = relabel[roster]
    orient = jax.random.randint(jax.random.fold_in(key, 22), (roster.shape[0], 1), 0, 2)
    reversed_pairs = labelled[:, ::-1]
    return jnp.where(orient == 1, reversed_pairs, labelled).astype(jnp.int32)


def steps_of(stream_key, extent, split, low, top_value):
    def one(dim, blocks):
        heights = jax.random.uniform(jax.random.fold_in(jax.random.fold_in(stream_key, 6), dim), (blocks,), jnp.float32, low / len(split), top_value / len(split))
        return jnp.repeat(jnp.exp(heights), extent[dim] // blocks).reshape((-1,) + (1,) * (len(extent) - dim - 1))

    gain = one(*split[0])
    for cut in split[1:]:
        gain = gain * one(*cut)
    return gain


def picks_of(rng, rows, amount, top, lift):
    order = jax.random.permutation(jax.random.fold_in(rng, 1), amount)
    favour = order
    for power in range(3):
        favour = favour * favour // amount
    favour = favour * lift // amount
    tickets = jax.random.randint(jax.random.fold_in(rng, 2), (rows, amount), 0, 4096) + favour
    holders = jax.random.permutation(jax.random.fold_in(rng, 3), rows)[jnp.arange(amount) % rows]
    tickets = jnp.where(jnp.arange(rows)[:, None] == holders[None, :], 1 << 14, tickets)
    score = tickets * amount + jnp.arange(amount)
    return lax.top_k(score.astype(jnp.int32), top)[1].astype(jnp.int32)


def scatter_about(key, extent, scale, most, held_as=jnp.bfloat16):
    result = jax.random.normal(key, extent, jnp.float32) * scale
    return jnp.minimum(jnp.maximum(result, -most), most).astype(held_as)


def setup_inputs(seed: int = 0) -> dict:
    streams_of = jax.random.split(jax.random.key(seed), 7)
    voltages = draw_voltages(jax.random.fold_in(streams_of[6], 71), 0)
    filter_taps = scatter_about(streams_of[1], (TAPS, NFFT), TAPS ** -0.5, 1.75, jnp.float32)
    beam_stations = picks_of(streams_of[2], BEAMS, STATIONS, LIST, 4096)
    beam_gain = jnp.clip(jnp.exp(math.log(4.0) - 2.7725887 * jax.random.uniform(streams_of[3], (BEAMS, LIST), jnp.float32) ** steps_of(streams_of[3], (BEAMS, LIST), ((0, 4),), -0.2, 0.2)), 0.25, 4.0)
    beam_delay = jnp.clip(jax.random.uniform(streams_of[4], (BEAMS, LIST), jnp.float32, -8.0, 8.0) * steps_of(streams_of[4], (BEAMS, LIST), ((0, 4),), -0.4, 0.0), -8.0, 8.0)
    block_pairs = draw_block_pairs(jax.random.fold_in(streams_of[6], 71), 0)
    return {"voltages": voltages, "filter_taps": filter_taps, "beam_stations": beam_stations, "beam_gain": beam_gain, "beam_delay": beam_delay, "block_pairs": block_pairs}


def channelize(filter_taps, group):
    samples = group.astype(jnp.float32)
    signal = filter_taps[0] * samples[:, 0:SPEC]
    for tap_index in range(1, TAPS):
        signal = signal + filter_taps[tap_index] * samples[:, tap_index:tap_index + SPEC]
    complex_signal = signal[:, :, 0, :] + 1j * signal[:, :, 1, :]
    transformed = jnp.fft.fft(complex_signal, axis=-1) / math.sqrt(NFFT)
    stacked = jnp.stack([jnp.real(transformed), jnp.imag(transformed)], axis=1)
    ordered = jnp.transpose(stacked, (0, 3, 1, 2))
    return ordered.reshape(group.shape[0], NFFT, 2 * SPEC).astype(jnp.bfloat16)

def reference(voltages, filter_taps, beam_stations, beam_gain, beam_delay, block_pairs):
    highest = lax.Precision.HIGHEST
    grouped = voltages.reshape(NBLK, BLK, FRAMES, 2, NFFT)
    spectra = lax.map(partial(channelize, filter_taps), grouped).reshape(INPUTS, NFFT, 2 * SPEC)
    wide = lax.optimization_barrier(spectra).astype(jnp.float32)
    channel_ids = jnp.arange(NFFT, dtype=jnp.int32).astype(jnp.float32)
    phases = 2.0 * math.pi / NFFT * beam_delay[:, :, None] * channel_ids[None, None, :]
    scaled = beam_gain / math.sqrt(LIST)
    weight_real = scaled[:, :, None] * jnp.cos(phases)
    weight_imag = -scaled[:, :, None] * jnp.sin(phases)
    beam_index = jnp.broadcast_to(jnp.arange(BEAMS, dtype=jnp.int32)[:, None], beam_stations.shape)
    empty = jnp.zeros((BEAMS, STATIONS, NFFT), jnp.float32)
    station_real = empty.at[beam_index, beam_stations].set(weight_real)
    station_imag = empty.at[beam_index, beam_stations].set(weight_imag)
    station_real = lax.optimization_barrier(station_real.astype(jnp.bfloat16)).astype(jnp.float32)
    station_imag = lax.optimization_barrier(station_imag.astype(jnp.bfloat16)).astype(jnp.float32)
    by_station = wide.reshape(STATIONS, 2, NFFT, 2 * SPEC)
    from_real = jnp.einsum('btc,tpcs->bpcs', station_real, by_station, precision=highest)
    from_imag = jnp.einsum('btc,tpcs->bpcs', station_imag, by_station, precision=highest)
    beam_real = from_real[..., :SPEC] - from_imag[..., SPEC:]
    beam_imag = from_real[..., SPEC:] + from_imag[..., :SPEC]
    beam_spectra = jnp.concatenate([beam_real, beam_imag], axis=-1).astype(jnp.bfloat16)
    scale = 1.0 / (FAVG * SPEC)
    contract_len = FAVG * 2 * SPEC

    def one_channel(out_index):
        start = (out_index * FAVG).astype(jnp.int32)
        channel_band = lax.dynamic_slice_in_dim(wide, start, FAVG, 1)
        blocks = channel_band.reshape(NBLK, BLK, contract_len)
        halves = channel_band.reshape(NBLK, BLK, FAVG, 2, SPEC)
        swapped = jnp.concatenate([halves[:, :, :, 1:2], -halves[:, :, :, 0:1]], axis=3)
        swapped = swapped.reshape(NBLK, BLK, contract_len)
        left_rows = blocks[block_pairs[:, 0]]
        left_swap = swapped[block_pairs[:, 0]]
        right_rows = blocks[block_pairs[:, 1]]
        real_vis = jnp.einsum('prm,pcm->prc', left_rows, right_rows, precision=highest)
        imag_vis = jnp.einsum('prm,pcm->prc', left_swap, right_rows, precision=highest)
        return (jnp.concatenate([real_vis, imag_vis], axis=-1) * scale).astype(jnp.bfloat16)
    visibilities = lax.map(one_channel, jnp.arange(OUTCH, dtype=jnp.int32))
    return (visibilities, beam_spectra)
```

```python
import functools
import math

import jax
import jax.numpy as jnp
import numpy as np
from jax import lax
from jax.experimental import pallas as pl
from jax.experimental.pallas import tpu as pltpu
from jax.sharding import PartitionSpec as P

STATIONS = 512
INPUTS = 1024
NFFT = 4096
BEAMS = 16
TAPS = 12
FAVG = 4
BLK = 64
LIST = 128
SPEC = 16
FRAMES = 27
NBLK = 16
PAIRS = 16
R1 = 32
R2 = 128
GROUPS = R1 // FAVG
OUTCH = NFFT // FAVG
SEND_GROUP = 2
F32 = jnp.float32
BF16 = jnp.bfloat16
NT = (((1,), (1,)), ((), ()))
TN = (((0,), (0,)), ((), ()))


def tables():
    b = np.arange(R2)
    ang = 2.0 * np.pi * (b[:, None] * b[None, :] % R2) / R2
    f2 = np.block([[np.cos(ang), np.sin(ang)], [-np.sin(ang), np.cos(ang)]])
    hi = f2.astype(jnp.bfloat16)
    lo = (f2 - hi.astype(np.float64)).astype(jnp.bfloat16)
    f2 = np.concatenate([hi, lo], axis=0)
    ang = 2.0 * np.pi * (np.arange(R1)[:, None] * b[None, :]) / NFFT
    tw = np.stack([np.cos(ang), -np.sin(ang)], axis=1) / math.sqrt(NFFT)
    ang = 2.0 * np.pi * (np.arange(8)[:, None] * np.arange(4)[None, :]) / R1
    mid = np.stack([np.cos(ang), -np.sin(ang)], axis=-1).reshape(8, 8, 1)
    mid = np.broadcast_to(mid, (8, 8, R2))
    return f2, tw.astype(np.float32), mid.astype(np.float32)


def add(x, y):
    return (x[0] + y[0], x[1] + y[1])


def sub(x, y):
    return (x[0] - y[0], x[1] - y[1])


def turn(x):
    return (x[1], -x[0])


def dft4(x):
    p, m = add(x[0], x[2]), sub(x[0], x[2])
    q, n = add(x[1], x[3]), turn(sub(x[1], x[3]))
    return [add(p, q), add(m, n), sub(p, q), sub(m, n)]


def dft8(x):
    even = dft4(x[0::2])
    odd = dft4(x[1::2])
    h = math.sqrt(0.5)
    o1, o3 = odd[1], odd[3]
    odd = [
        odd[0],
        ((o1[0] + o1[1]) * h, (o1[1] - o1[0]) * h),
        turn(odd[2]),
        ((o3[1] - o3[0]) * h, -(o3[0] + o3[1]) * h),
    ]
    return [add(e, o) for e, o in zip(even, odd)] + [sub(e, o) for e, o in zip(even, odd)]


def transform(group, step, v_ref, taps_ref, tw_ref, mtw_ref, f2_ref, vs, mid, y_hi, y_lo, os):
    rows = vs.reshape(2 * R1 * 32, R2)
    for frame in range(FRAMES):
        rows[pl.ds(frame, 2 * R1, stride=32), :] = v_ref[frame].astype(F32)

    def low(a_lo, carry):
        x = []
        for a_hi in range(4):
            a = a_lo + 8 * a_hi
            parts = [None, None]
            for t in range(TAPS):
                tap = taps_ref[t : t + 1, pl.ds(pl.multiple_of(a * R2, R2), R2)]
                for q in range(2):
                    term = tap * vs[2 * a + q, t : t + SPEC, :]
                    parts[q] = term if t == 0 else parts[q] + term
            x.append(tuple(parts))
        z = dft4(x)
        for k in range(4):
            zr, zi = z[k]
            if k:
                wr = mtw_ref[a_lo, 2 * k : 2 * k + 1, :]
                wi = mtw_ref[a_lo, 2 * k + 1 : 2 * k + 2, :]
                zr, zi = zr * wr - zi * wi, zr * wi + zi * wr
            mid[k, 2 * a_lo] = zr
            mid[k, 2 * a_lo + 1] = zi
        return carry

    lax.fori_loop(0, 8, low, 0)
    for k in range(4):
        z = dft8([(mid[k, 2 * a], mid[k, 2 * a + 1]) for a in range(8)])
        for k2 in range(8):
            c1 = k + 4 * k2
            zr, zi = z[k2]
            wr, wi = tw_ref[c1, 0:1, :], tw_ref[c1, 1:2, :]
            for q, val in enumerate((zr * wr - zi * wi, zr * wi + zi * wr)):
                hi = val.astype(BF16)
                y_hi[c1 * SPEC : (c1 + 1) * SPEC, q * R2 : (q + 1) * R2] = hi
                y_lo[c1 * SPEC : (c1 + 1) * SPEC, q * R2 : (q + 1) * R2] = (
                    val - hi.astype(F32)
                ).astype(BF16)
    left = lax.broadcasted_iota(jnp.int32, (R2, R2), 1) < 64
    for h in range(2):
        yh = y_hi[h * 256 : (h + 1) * 256, :]
        yl = y_lo[h * 256 : (h + 1) * 256, :]
        full = lax.dot_general(f2_ref[...], yh, NT, preferred_element_type=F32)
        res = full[0:256] + full[256:512]
        res = res + lax.dot_general(f2_ref[0:256, :], yl, NT, preferred_element_type=F32)
        for j in range(2):
            re = res[0:R2, j * R2 : (j + 1) * R2]
            im = res[R2 : 2 * R2, j * R2 : (j + 1) * R2]
            first = jnp.where(left, re, pltpu.roll(im, 64, 1))
            second = jnp.where(left, pltpu.roll(re, 64, 1), im)
            g = 4 * h + 2 * j
            os[pl.ds(g * group + step, R2, stride=GROUPS * group), :] = first
            os[pl.ds((g + 1) * group + step, R2, stride=GROUPS * group), :] = second


def fft_kernel(group, v_ref, taps_ref, tw_ref, mtw_ref, f2_ref, out_ref, vs, mid, y_hi, y_lo, os):
    step = pl.program_id(1)
    transform(group, step, v_ref, taps_ref, tw_ref, mtw_ref, f2_ref, vs, mid, y_hi, y_lo, os)

    @pl.when(step == group - 1)
    def _():
        n_dest, per_dest = out_ref.shape[0], out_ref.shape[1]

        def emit(dest, carry):
            size = per_dest * group
            part = os[pl.ds(pl.multiple_of(dest * size, size), size), :]
            out_ref[dest] = part.reshape(per_dest, group, R2).astype(BF16)
            return carry

        lax.fori_loop(0, n_dest, emit, 0)


def by_sample(voltages):
    count = voltages.shape[0]
    split = voltages.reshape(count, FRAMES, 2, R1, R2)
    return jnp.transpose(split, (0, 1, 3, 2, 4)).reshape(count, FRAMES, 2 * R1, R2)


def channelize(voltages, filter_taps, devices):
    count = voltages.shape[0]
    group = min(16, count)
    per_dest = OUTCH // devices
    f2, tw, mtw = tables()
    return pl.pallas_call(
        functools.partial(fft_kernel, group),
        grid=(count // group, group),
        out_shape=jax.ShapeDtypeStruct((devices, per_dest, count, R2), BF16),
        in_specs=[
            pl.BlockSpec((None, FRAMES, 2 * R1, R2), lambda i, j: (i * group + j, 0, 0, 0)),
            pl.BlockSpec((TAPS, NFFT), lambda i, j: (0, 0)),
            pl.BlockSpec((R1, 2, R2), lambda i, j: (0, 0, 0)),
            pl.BlockSpec((8, 8, R2), lambda i, j: (0, 0, 0)),
            pl.BlockSpec((512, 256), lambda i, j: (0, 0)),
        ],
        out_specs=pl.BlockSpec((devices, per_dest, group, R2), lambda i, j: (0, 0, i, 0)),
        scratch_shapes=[
            pltpu.VMEM((2 * R1, 32, R2), F32),
            pltpu.VMEM((4, 16, SPEC, R2), F32),
            pltpu.VMEM((512, 256), BF16),
            pltpu.VMEM((512, 256), BF16),
            pltpu.VMEM((OUTCH * group, R2), F32),
        ],
        compiler_params=pltpu.CompilerParams(vmem_limit_bytes=48 << 20),
        name="channelize",
    )(
        by_sample(voltages),
        filter_taps,
        jnp.asarray(tw),
        jnp.asarray(mtw),
        jnp.asarray(f2),
    )


def send_kernel(
    stn, chan, group, v_ref, taps_ref, tw_ref, mtw_ref, f2_ref, gain, delay, dst, gains, delays,
    vs, mid, y_hi, y_lo, os, stage, send_sem, recv_sem, own_sem, beam_send, beam_recv, beam_own,
):
    devices = stn * chan
    me = lax.axis_index("stn") * chan + lax.axis_index("chan")
    part, step = pl.program_id(0), pl.program_id(1)
    parts = stage.shape[0]
    per_dest = stage.shape[2]
    barrier = pltpu.get_barrier_semaphore()

    def peer(k):
        dest = lax.rem(me + k, devices)
        return dest, (dest // chan, lax.rem(dest, chan))

    row = lax.axis_index("stn")
    column = lax.axis_index("chan")
    small = ((gain, gains), (delay, delays))

    def beam_copy(which, k):
        return pltpu.make_async_remote_copy(
            src_ref=small[which][0],
            dst_ref=small[which][1].at[row],
            send_sem=beam_send.at[which, k],
            recv_sem=beam_recv.at[which, k],
            device_id=(lax.rem(row + k, stn), column),
            device_id_type=pl.DeviceIdType.MESH,
        )

    def beam_keep(which):
        return pltpu.make_async_copy(small[which][0], small[which][1].at[row], beam_own.at[which])

    @pl.when((part == 0) & (step == 0))
    def _():
        def greet(k, carry):
            pl.semaphore_signal(
                barrier, inc=1, device_id=peer(k)[1], device_id_type=pl.DeviceIdType.MESH
            )
            return carry

        lax.fori_loop(1, devices, greet, 0)

    transform(group, step, v_ref, taps_ref, tw_ref, mtw_ref, f2_ref, vs, mid, y_hi, y_lo, os)

    @pl.when((part == 0) & (step == group - 1))
    def _():
        pl.semaphore_wait(barrier, devices - 1)
        for which in range(2):
            for k in range(1, stn):
                beam_copy(which, k).start()
            beam_keep(which).start()

    def place(which):
        return dst.at[:, pl.ds(me * parts + which, 1)]

    def copy(which, k):
        dest, where = peer(k)
        return pltpu.make_async_remote_copy(
            src_ref=stage.at[which, dest],
            dst_ref=place(which),
            send_sem=send_sem.at[which, k],
            recv_sem=recv_sem.at[which, k],
            device_id=where,
            device_id_type=pl.DeviceIdType.MESH,
        )

    def own(which):
        return pltpu.make_async_copy(stage.at[which, me], place(which), own_sem.at[which])

    def fill(dest):
        size = per_dest * group
        rows = os[pl.ds(pl.multiple_of(dest * size, size), size), :]
        stage[part, dest] = rows.reshape(per_dest, 1, group, R2).astype(BF16)

    @pl.when(step == group - 1)
    def _():
        def emit(k, carry):
            fill(peer(k)[0])
            copy(part, k).start()
            return carry

        lax.fori_loop(1, devices, emit, 0)
        fill(me)
        own(part).start()

    @pl.when((part == parts - 1) & (step == group - 1))
    def _():
        def finish(n, carry):
            copy(n // (devices - 1), 1 + lax.rem(n, devices - 1)).wait()
            return carry

        lax.fori_loop(0, parts * (devices - 1), finish, 0)
        for which in range(parts):
            own(which).wait()
        for which in range(2):
            for k in range(1, stn):
                beam_copy(which, k).wait()
            beam_keep(which).wait()


def spectra_of_channels(voltages, filter_taps, gain, delay, stn, chan):
    count = voltages.shape[0]
    devices = stn * chan
    per_dest = OUTCH // devices
    if count % SEND_GROUP:
        spectra = channelize(voltages, filter_taps, devices)
        moved = lax.all_to_all(spectra, ("stn", "chan"), split_axis=0, concat_axis=0, tiled=True)
        turned = jnp.transpose(moved, (1, 0, 2, 3)).reshape(per_dest, devices * count, R2)
        gains = lax.all_gather(gain, "stn", axis=0, tiled=True)
        delays = lax.all_gather(delay, "stn", axis=0, tiled=True)
        return turned, gains, delays
    group = SEND_GROUP
    parts = count // group
    f2, tw, mtw = tables()
    turned, gains, delays = pl.pallas_call(
        functools.partial(send_kernel, stn, chan, group),
        grid=(parts, group),
        out_shape=[
            jax.ShapeDtypeStruct((per_dest, devices * parts, group, R2), BF16),
            jax.ShapeDtypeStruct((stn,) + gain.shape, F32),
            jax.ShapeDtypeStruct((stn,) + delay.shape, F32),
        ],
        in_specs=[
            pl.BlockSpec((None, FRAMES, 2 * R1, R2), lambda i, j: (i * group + j, 0, 0, 0)),
            pl.BlockSpec((TAPS, NFFT), lambda i, j: (0, 0)),
            pl.BlockSpec((R1, 2, R2), lambda i, j: (0, 0, 0)),
            pl.BlockSpec((8, 8, R2), lambda i, j: (0, 0, 0)),
            pl.BlockSpec((512, 256), lambda i, j: (0, 0)),
            pl.BlockSpec(memory_space=pl.ANY),
            pl.BlockSpec(memory_space=pl.ANY),
        ],
        out_specs=[pl.BlockSpec(memory_space=pl.ANY)] * 3,
        scratch_shapes=[
            pltpu.VMEM((2 * R1, 32, R2), F32),
            pltpu.VMEM((4, 16, SPEC, R2), F32),
            pltpu.VMEM((512, 256), BF16),
            pltpu.VMEM((512, 256), BF16),
            pltpu.VMEM((OUTCH * group, R2), F32),
            pltpu.VMEM((parts, devices, per_dest, 1, group, R2), BF16),
            pltpu.SemaphoreType.DMA((parts, devices)),
            pltpu.SemaphoreType.DMA((parts, devices)),
            pltpu.SemaphoreType.DMA((parts,)),
            pltpu.SemaphoreType.DMA((2, stn)),
            pltpu.SemaphoreType.DMA((2, stn)),
            pltpu.SemaphoreType.DMA((2,)),
        ],
        compiler_params=pltpu.CompilerParams(
            vmem_limit_bytes=60 << 20, collective_id=0, has_side_effects=True
        ),
        cost_estimate=pl.CostEstimate(flops=10**11, bytes_accessed=1 << 28, transcendentals=0),
        name="channelize_send",
    )(
        by_sample(voltages),
        filter_taps,
        jnp.asarray(tw),
        jnp.asarray(mtw),
        jnp.asarray(f2),
        gain,
        delay,
    )
    turned = turned.reshape(per_dest, devices * count, R2)
    return turned, gains.reshape(BEAMS, LIST), delays.reshape(BEAMS, LIST)


def correlate_kernel(pairs, x_ref, wr_ref, wi_ref, vis_ref, beam_ref, both, wide, sums):
    chunk = pl.program_id(0)
    some = x_ref.shape[0]
    lane = lax.broadcasted_iota(jnp.int32, (1, R2), 1)
    sign = jnp.where(lane < 64, -1.0, 1.0).astype(F32)
    of = (lane // SPEC) % FAVG
    for o in range(some):
        for k in range(NBLK):
            x = x_ref[o, k * BLK : (k + 1) * BLK, :]
            xf = x.astype(F32)
            wide[o, k * BLK : (k + 1) * BLK, :] = xf
            both[o, k, 0:BLK, :] = x
            both[o, k, BLK : 2 * BLK, :] = (pltpu.roll(xf, 64, 1) * sign).astype(BF16)
        for r in range(PAIRS):
            rows = both[o, pairs[0, r], 0:BLK, :]
            vis = lax.dot_general(rows, both[o, pairs[1, r]], NT, preferred_element_type=F32)
            vis_ref[o, r] = (vis * (1.0 / (FAVG * SPEC))).astype(BF16)
        for p in range(2):
            x = wide.at[o][pl.ds(p, STATIONS, stride=2), :].astype(BF16)
            real = jnp.dot(wr_ref[o], x, preferred_element_type=F32)
            imag = jnp.dot(wi_ref[o], x, preferred_element_type=F32)
            beams = real + sign * pltpu.roll(imag, 64, 1)
            total = beams[0:BEAMS]
            for f in range(1, FAVG):
                total = jnp.where(of == f, beams[f * BEAMS : (f + 1) * BEAMS], total)
            first = pl.multiple_of(((chunk * some + o) * 2 + p) * BEAMS, BEAMS)
            sums[pl.ds(first, BEAMS), :] = total

    @pl.when(chunk == pl.num_programs(0) - 1)
    def _():
        turn_beams(sums, beam_ref)


def turn_beams(sums, beam_ref):
    lanes = beam_ref.shape[3]
    count = lanes // FAVG
    column = lax.broadcasted_iota(jnp.int32, (count, lanes), 1)
    spread = jnp.where(column // FAVG == lax.broadcasted_iota(jnp.int32, (count, lanes), 0), 1.0, 0.0)
    spread = spread.astype(BF16)
    fine = lax.broadcasted_iota(jnp.int32, (1, lanes), 1) % FAVG
    for p in range(2):
        for b in range(BEAMS):
            rows = sums[pl.ds(p * BEAMS + b, count, stride=2 * BEAMS), :].astype(BF16)
            moved = lax.dot_general(rows, spread, TN, preferred_element_type=F32)
            for q in range(2):
                total = moved[q * 64 : q * 64 + SPEC]
                for f in range(1, FAVG):
                    total = jnp.where(fine == f, moved[q * 64 + f * SPEC : q * 64 + (f + 1) * SPEC], total)
                beam_ref[b, p, q * SPEC : (q + 1) * SPEC, :] = total.astype(BF16)


def correlate(turned, real, imag, block_pairs):
    per_dest = turned.shape[0]
    lanes = FAVG * per_dest
    some = math.gcd(per_dest, 4)
    weight_spec = pl.BlockSpec((some, FAVG * BEAMS, STATIONS), lambda o, pairs: (o, 0, 0))
    visibilities, beams = pl.pallas_call(
        correlate_kernel,
        grid_spec=pltpu.PrefetchScalarGridSpec(
            num_scalar_prefetch=1,
            grid=(per_dest // some,),
            in_specs=[
                pl.BlockSpec((some, INPUTS, R2), lambda o, pairs: (o, 0, 0)),
                weight_spec,
                weight_spec,
            ],
            out_specs=[
                pl.BlockSpec((some, PAIRS, BLK, 2 * BLK), lambda o, pairs: (o, 0, 0, 0)),
                pl.BlockSpec((BEAMS, 2, 2 * SPEC, lanes), lambda o, pairs: (0, 0, 0, 0)),
            ],
            scratch_shapes=[
                pltpu.VMEM((some, NBLK, 2 * BLK, R2), BF16),
                pltpu.VMEM((some, INPUTS, R2), F32),
                pltpu.VMEM((per_dest * 2 * BEAMS, R2), F32),
            ],
        ),
        out_shape=[
            jax.ShapeDtypeStruct((per_dest, PAIRS, BLK, 2 * BLK), BF16),
            jax.ShapeDtypeStruct((BEAMS, 2, 2 * SPEC, lanes), BF16),
        ],
        name="correlate",
    )(block_pairs.T, turned, real, imag)
    return visibilities, jnp.swapaxes(beams, 2, 3)


def beam_weights(stations, gains, delays, chan_start, per_dest):
    named = stations[:, :, None] == jnp.arange(STATIONS, dtype=jnp.int32)[None, None, :]
    gain = jnp.sum(jnp.where(named, gains[:, :, None] / math.sqrt(LIST), 0.0), axis=1)
    delay = jnp.sum(jnp.where(named, delays[:, :, None], 0.0), axis=1)
    rate = 2.0 * math.pi / NFFT * delay
    coarse = (chan_start + FAVG * jnp.arange(per_dest, dtype=jnp.int32)).astype(F32)
    base = rate[None] * coarse[:, None, None]
    base_cos, base_sin = gain * jnp.cos(base), gain * jnp.sin(base)
    fine = rate[None] * jnp.arange(FAVG, dtype=jnp.int32).astype(F32)[:, None, None]
    fine_cos, fine_sin = jnp.cos(fine)[None], jnp.sin(fine)[None]
    base_cos, base_sin = base_cos[:, None], base_sin[:, None]
    real = base_cos * fine_cos - base_sin * fine_sin
    imag = -(base_sin * fine_cos + base_cos * fine_sin)
    shape = (per_dest, FAVG * BEAMS, STATIONS)
    return real.astype(BF16).reshape(shape), imag.astype(BF16).reshape(shape)


def shards(voltages, filter_taps, beam_stations, beam_gain, beam_delay, block_pairs):
    stn = lax.axis_size("stn")
    chan = lax.axis_size("chan")
    devices = stn * chan
    per_dest = OUTCH // devices
    chan_start = (lax.axis_index("stn") * chan + lax.axis_index("chan")) * (NFFT // devices)
    turned, gains, delays = spectra_of_channels(
        voltages, filter_taps, beam_gain, beam_delay, stn, chan
    )
    real, imag = beam_weights(beam_stations, gains, delays, chan_start, per_dest)
    return correlate(turned, real, imag, block_pairs)


def solution(mesh):
    placed = (P(("stn", "chan"), None, None, None), P(), P(), P("stn", None), P("stn", None), P())
    return jax.shard_map(
        shards,
        mesh=mesh,
        in_specs=placed,
        out_specs=(P(("stn", "chan"), None, None, None), P(None, None, ("stn", "chan"), None)),
        check_vma=False,
    )
```

```python
import functools
import math

import jax
import jax.numpy as jnp
import numpy as np
from jax import lax
from jax.experimental import pallas as pl
from jax.experimental.pallas import tpu as pltpu
from jax.sharding import PartitionSpec as P

STATIONS = 512
INPUTS = 1024
NFFT = 4096
BEAMS = 16
TAPS = 12
FAVG = 4
BLK = 64
LIST = 128
SPEC = 16
FRAMES = 27
NBLK = 16
PAIRS = 16
R1 = 32
R2 = 128
GROUPS = R1 // FAVG
OUTCH = NFFT // FAVG
SEND_GROUP = 2
LATE = 8
CHUNK = 4
F32 = jnp.float32
BF16 = jnp.bfloat16
NT = (((1,), (1,)), ((), ()))
TN = (((0,), (0,)), ((), ()))


def tables():
    b = np.arange(R2)
    ang = 2.0 * np.pi * (b[:, None] * b[None, :] % R2) / R2
    f2 = np.block([[np.cos(ang), np.sin(ang)], [-np.sin(ang), np.cos(ang)]])
    hi = f2.astype(jnp.bfloat16)
    lo = (f2 - hi.astype(np.float64)).astype(jnp.bfloat16)
    f2 = np.concatenate([hi, lo], axis=0)
    ang = 2.0 * np.pi * (np.arange(R1)[:, None] * b[None, :]) / NFFT
    tw = np.stack([np.cos(ang), -np.sin(ang)], axis=1) / math.sqrt(NFFT)
    ang = 2.0 * np.pi * (np.arange(8)[:, None] * np.arange(4)[None, :]) / R1
    mid = np.stack([np.cos(ang), -np.sin(ang)], axis=-1).reshape(8, 8, 1)
    mid = np.broadcast_to(mid, (8, 8, R2))
    return f2, tw.astype(np.float32), mid.astype(np.float32)


def add(x, y):
    return (x[0] + y[0], x[1] + y[1])


def sub(x, y):
    return (x[0] - y[0], x[1] - y[1])


def turn(x):
    return (x[1], -x[0])


def dft4(x):
    p, m = add(x[0], x[2]), sub(x[0], x[2])
    q, n = add(x[1], x[3]), turn(sub(x[1], x[3]))
    return [add(p, q), add(m, n), sub(p, q), sub(m, n)]


def dft8(x):
    even = dft4(x[0::2])
    odd = dft4(x[1::2])
    h = math.sqrt(0.5)
    o1, o3 = odd[1], odd[3]
    odd = [
        odd[0],
        ((o1[0] + o1[1]) * h, (o1[1] - o1[0]) * h),
        turn(odd[2]),
        ((o3[1] - o3[0]) * h, -(o3[0] + o3[1]) * h),
    ]
    return [add(e, o) for e, o in zip(even, odd)] + [sub(e, o) for e, o in zip(even, odd)]


def transform(group, step, v_ref, taps_ref, tw_ref, mtw_ref, f2_ref, vs, mid, y_hi, y_lo, os):
    rows = vs.reshape(2 * R1 * 32, R2)
    for frame in range(FRAMES):
        rows[pl.ds(frame, 2 * R1, stride=32), :] = v_ref[frame].astype(F32)

    def low(a_lo, carry):
        x = []
        for a_hi in range(4):
            a = a_lo + 8 * a_hi
            parts = [None, None]
            for t in range(TAPS):
                tap = taps_ref[t : t + 1, pl.ds(pl.multiple_of(a * R2, R2), R2)]
                for q in range(2):
                    term = tap * vs[2 * a + q, t : t + SPEC, :]
                    parts[q] = term if t == 0 else parts[q] + term
            x.append(tuple(parts))
        z = dft4(x)
        for k in range(4):
            zr, zi = z[k]
            if k:
                wr = mtw_ref[a_lo, 2 * k : 2 * k + 1, :]
                wi = mtw_ref[a_lo, 2 * k + 1 : 2 * k + 2, :]
                zr, zi = zr * wr - zi * wi, zr * wi + zi * wr
            mid[k, 2 * a_lo] = zr
            mid[k, 2 * a_lo + 1] = zi
        return carry

    lax.fori_loop(0, 8, low, 0)
    for k in range(4):
        z = dft8([(mid[k, 2 * a], mid[k, 2 * a + 1]) for a in range(8)])
        for k2 in range(8):
            c1 = k + 4 * k2
            zr, zi = z[k2]
            wr, wi = tw_ref[c1, 0:1, :], tw_ref[c1, 1:2, :]
            for q, val in enumerate((zr * wr - zi * wi, zr * wi + zi * wr)):
                hi = val.astype(BF16)
                y_hi[c1 * SPEC : (c1 + 1) * SPEC, q * R2 : (q + 1) * R2] = hi
                y_lo[c1 * SPEC : (c1 + 1) * SPEC, q * R2 : (q + 1) * R2] = (
                    val - hi.astype(F32)
                ).astype(BF16)
    left = lax.broadcasted_iota(jnp.int32, (R2, R2), 1) < 64
    for h in range(2):
        yh = y_hi[h * 256 : (h + 1) * 256, :]
        yl = y_lo[h * 256 : (h + 1) * 256, :]
        full = lax.dot_general(f2_ref[...], yh, NT, preferred_element_type=F32)
        res = full[0:256] + full[256:512]
        res = res + lax.dot_general(f2_ref[0:256, :], yl, NT, preferred_element_type=F32)
        for j in range(2):
            re = res[0:R2, j * R2 : (j + 1) * R2]
            im = res[R2 : 2 * R2, j * R2 : (j + 1) * R2]
            first = jnp.where(left, re, pltpu.roll(im, 64, 1))
            second = jnp.where(left, pltpu.roll(re, 64, 1), im)
            g = 4 * h + 2 * j
            os[pl.ds(g * group + step, R2, stride=GROUPS * group), :] = first
            os[pl.ds((g + 1) * group + step, R2, stride=GROUPS * group), :] = second


def fft_kernel(group, v_ref, taps_ref, tw_ref, mtw_ref, f2_ref, out_ref, vs, mid, y_hi, y_lo, os):
    step = pl.program_id(1)
    transform(group, step, v_ref, taps_ref, tw_ref, mtw_ref, f2_ref, vs, mid, y_hi, y_lo, os)

    @pl.when(step == group - 1)
    def _():
        n_dest, per_dest = out_ref.shape[0], out_ref.shape[1]

        def emit(dest, carry):
            size = per_dest * group
            part = os[pl.ds(pl.multiple_of(dest * size, size), size), :]
            out_ref[dest] = part.reshape(per_dest, group, R2).astype(BF16)
            return carry

        lax.fori_loop(0, n_dest, emit, 0)


def by_sample(voltages):
    count = voltages.shape[0]
    split = voltages.reshape(count, FRAMES, 2, R1, R2)
    return jnp.transpose(split, (0, 1, 3, 2, 4)).reshape(count, FRAMES, 2 * R1, R2)


def channelize(voltages, filter_taps, devices):
    count = voltages.shape[0]
    group = min(16, count)
    per_dest = OUTCH // devices
    f2, tw, mtw = tables()
    return pl.pallas_call(
        functools.partial(fft_kernel, group),
        grid=(count // group, group),
        out_shape=jax.ShapeDtypeStruct((devices, per_dest, count, R2), BF16),
        in_specs=[
            pl.BlockSpec((None, FRAMES, 2 * R1, R2), lambda i, j: (i * group + j, 0, 0, 0)),
            pl.BlockSpec((TAPS, NFFT), lambda i, j: (0, 0)),
            pl.BlockSpec((R1, 2, R2), lambda i, j: (0, 0, 0)),
            pl.BlockSpec((8, 8, R2), lambda i, j: (0, 0, 0)),
            pl.BlockSpec((512, 256), lambda i, j: (0, 0)),
        ],
        out_specs=pl.BlockSpec((devices, per_dest, group, R2), lambda i, j: (0, 0, i, 0)),
        scratch_shapes=[
            pltpu.VMEM((2 * R1, 32, R2), F32),
            pltpu.VMEM((4, 16, SPEC, R2), F32),
            pltpu.VMEM((512, 256), BF16),
            pltpu.VMEM((512, 256), BF16),
            pltpu.VMEM((OUTCH * group, R2), F32),
        ],
        compiler_params=pltpu.CompilerParams(vmem_limit_bytes=48 << 20),
        name="channelize",
    )(
        by_sample(voltages),
        filter_taps,
        jnp.asarray(tw),
        jnp.asarray(mtw),
        jnp.asarray(f2),
    )


def steer(first_channel, stations, gains, delays, wr, wi):
    highest = lax.Precision.HIGHEST
    table = jnp.concatenate([gains / math.sqrt(LIST), delays * (2.0 * math.pi / NFFT)], axis=0)
    beam = lax.broadcasted_iota(jnp.int32, (2 * BEAMS, 1), 0) % BEAMS
    spread = jnp.zeros((2 * BEAMS, STATIONS), F32)
    for b in range(BEAMS):
        named = lax.broadcasted_iota(jnp.int32, (STATIONS, LIST), 0) == stations[b : b + 1, :]
        row = jnp.where(beam == b, table, 0.0)
        spread += lax.dot_general(
            row, named.astype(F32), NT, precision=highest, preferred_element_type=F32
        )
    gain, rate = spread[0:BEAMS], spread[BEAMS:]
    fine = [(jnp.cos(rate * float(f)), jnp.sin(rate * float(f))) for f in range(FAVG)]

    def one(o, carry):
        base = rate * (first_channel + FAVG * o).astype(F32)
        base_cos, base_sin = gain * jnp.cos(base), gain * jnp.sin(base)
        for f, (fine_cos, fine_sin) in enumerate(fine):
            real = base_cos * fine_cos - base_sin * fine_sin
            imag = -(base_sin * fine_cos + base_cos * fine_sin)
            wr[o, f * BEAMS : (f + 1) * BEAMS, :] = real.astype(BF16)
            wi[o, f * BEAMS : (f + 1) * BEAMS, :] = imag.astype(BF16)
        return carry

    lax.fori_loop(0, wr.shape[0], one, 0)


def station_kernel(
    stn, chan, v_ref, taps_ref, tw_ref, mtw_ref, f2_ref, pairs, stations, gain, delay, vis_ref, beam_ref,
    vs, mid, y_hi, y_lo, os, stage, x, gains, delays, wr, wi, both, wide, sums,
    send_sem, early_sem, late_sem, own_sem, beam_send, beam_recv, beam_own,
):
    devices = stn * chan
    row, column = lax.axis_index("stn"), lax.axis_index("chan")
    me = row * chan + column
    now = pl.program_id(0)
    per_dest, parts = stage.shape[1], stage.shape[2]
    count = parts * SEND_GROUP
    late = LATE // SEND_GROUP
    early = parts - late
    some = vis_ref.shape[0]
    chunks = per_dest // some
    part, step = now // SEND_GROUP, now % SEND_GROUP
    barrier = pltpu.get_barrier_semaphore()
    small = ((gain, gains), (delay, delays))

    def peer(k):
        dest = lax.rem(me + k, devices)
        return dest, (dest // chan, lax.rem(dest, chan))

    def beam_copy(which, k):
        return pltpu.make_async_remote_copy(
            src_ref=small[which][0],
            dst_ref=small[which][1].at[row],
            send_sem=beam_send.at[which, k],
            recv_sem=beam_recv.at[which, k],
            device_id=(lax.rem(row + k, stn), column),
            device_id_type=pl.DeviceIdType.MESH,
        )

    def beam_keep(which):
        return pltpu.make_async_copy(small[which][0], small[which][1].at[row], beam_own.at[which])

    def copy(k, outs, first, size, sem):
        dest, where = peer(k)
        return pltpu.make_async_remote_copy(
            src_ref=stage.at[dest, outs, pl.ds(first, size)],
            dst_ref=x.at[outs, pl.ds(me * parts + first, size)],
            send_sem=send_sem,
            recv_sem=sem,
            device_id=where,
            device_id_type=pl.DeviceIdType.MESH,
        )

    def own():
        return pltpu.make_async_copy(stage.at[me], x.at[:, pl.ds(me * parts, parts)], own_sem)

    def arrived(outs, size, sem):
        ref = x.at[outs, pl.ds(0, (devices - 1) * size)]
        pltpu.make_async_copy(ref, ref, sem).wait()

    def fill(dest):
        size = per_dest * SEND_GROUP
        rows = os[pl.ds(pl.multiple_of(dest * size, size), size), :]
        stage[dest, :, pl.ds(part, 1)] = rows.reshape(per_dest, 1, SEND_GROUP, R2).astype(BF16)

    @pl.when(now == 0)
    def _():
        def greet(k, carry):
            pl.semaphore_signal(
                barrier, inc=1, device_id=peer(k)[1], device_id_type=pl.DeviceIdType.MESH
            )
            return carry

        lax.fori_loop(1, devices, greet, 0)

    @pl.when(now < count)
    def _():
        transform(SEND_GROUP, step, v_ref, taps_ref, tw_ref, mtw_ref, f2_ref, vs, mid, y_hi, y_lo, os)

    @pl.when(now == SEND_GROUP - 1)
    def _():
        pl.semaphore_wait(barrier, devices - 1)
        for which in range(2):
            for k in range(1, stn):
                beam_copy(which, k).start()
            beam_keep(which).start()

    @pl.when((now < count) & (step == SEND_GROUP - 1) & (part < early))
    def _():
        def emit(k, carry):
            fill(peer(k)[0])
            copy(k, slice(None), part, 1, early_sem).start()
            return carry

        lax.fori_loop(1, devices, emit, 0)
        fill(me)

    @pl.when((now < count) & (step == SEND_GROUP - 1) & (part >= early))
    def _():
        def emit(dest, carry):
            fill(dest)
            return carry

        lax.fori_loop(0, devices, emit, 0)

    @pl.when(now == count - 1)
    def _():
        def emit(n, carry):
            chunk, k = n // (devices - 1), 1 + lax.rem(n, devices - 1)
            copy(k, pl.ds(chunk * some, some), early, late, late_sem.at[chunk]).start()
            return carry

        lax.fori_loop(0, chunks * (devices - 1), emit, 0)
        own().start()
        for which in range(2):
            for k in range(1, stn):
                beam_copy(which, k).wait()
            beam_keep(which).wait()
        every = [jnp.concatenate([ref[r] for r in range(stn)], axis=0) for ref in (gains, delays)]
        steer(me * (per_dest * FAVG), stations[...], every[0], every[1], wr, wi)
        own().wait()
        arrived(slice(None), early, early_sem)

    @pl.when(now >= count)
    def _():
        chunk = now - count
        arrived(pl.ds(chunk * some, some), late, late_sem.at[chunk])
        correlate_chunk(chunk, pairs, x, wr, wi, vis_ref, both, wide, sums)

    @pl.when(now == count + chunks - 1)
    def _():
        turn_beams(sums, beam_ref)
        sent = stage.at[pl.ds(0, devices - 1)]
        pltpu.make_async_copy(sent, sent, send_sem).wait()


def correlate_chunk(chunk, pairs, x_ref, wr_ref, wi_ref, vis_ref, both, wide, sums):
    some = vis_ref.shape[0]
    lane = lax.broadcasted_iota(jnp.int32, (1, R2), 1)
    sign = jnp.where(lane < 64, -1.0, 1.0).astype(F32)
    of = (lane // SPEC) % FAVG
    for o in range(some):
        out = chunk * some + o
        for k in range(NBLK):
            x = x_ref[out, k * BLK // 2 : (k + 1) * BLK // 2].reshape(BLK, R2)
            xf = x.astype(F32)
            wide[o, k * BLK : (k + 1) * BLK, :] = xf
            both[o, k, 0:BLK, :] = x
            both[o, k, BLK : 2 * BLK, :] = (pltpu.roll(xf, 64, 1) * sign).astype(BF16)
        for r in range(PAIRS):
            rows = both[o, pairs[0, r], 0:BLK, :]
            vis = lax.dot_general(rows, both[o, pairs[1, r]], NT, preferred_element_type=F32)
            vis_ref[o, r] = (vis * (1.0 / (FAVG * SPEC))).astype(BF16)
        for p in range(2):
            x = wide.at[o][pl.ds(p, STATIONS, stride=2), :].astype(BF16)
            real = jnp.dot(wr_ref[out], x, preferred_element_type=F32)
            imag = jnp.dot(wi_ref[out], x, preferred_element_type=F32)
            beams = real + sign * pltpu.roll(imag, 64, 1)
            total = beams[0:BEAMS]
            for f in range(1, FAVG):
                total = jnp.where(of == f, beams[f * BEAMS : (f + 1) * BEAMS], total)
            first = pl.multiple_of((out * 2 + p) * BEAMS, BEAMS)
            sums[pl.ds(first, BEAMS), :] = total


def fused(voltages, filter_taps, stations, gain, delay, block_pairs, stn, chan):
    count = voltages.shape[0]
    devices = stn * chan
    per_dest = OUTCH // devices
    parts = count // SEND_GROUP
    some = CHUNK
    chunks = per_dest // some
    lanes = FAVG * per_dest
    f2, tw, mtw = tables()
    visibilities, beams = pl.pallas_call(
        functools.partial(station_kernel, stn, chan),
        grid=(count + chunks,),
        out_shape=[
            jax.ShapeDtypeStruct((per_dest, PAIRS, BLK, 2 * BLK), BF16),
            jax.ShapeDtypeStruct((BEAMS, 2, 2 * SPEC, lanes), BF16),
        ],
        in_specs=[
            pl.BlockSpec((None, FRAMES, 2 * R1, R2), lambda i: (jnp.minimum(i, count - 1), 0, 0, 0)),
            pl.BlockSpec((TAPS, NFFT), lambda i: (0, 0)),
            pl.BlockSpec((R1, 2, R2), lambda i: (0, 0, 0)),
            pl.BlockSpec((8, 8, R2), lambda i: (0, 0, 0)),
            pl.BlockSpec((512, 256), lambda i: (0, 0)),
            pl.BlockSpec(memory_space=pltpu.SMEM),
            pl.BlockSpec((BEAMS, LIST), lambda i: (0, 0)),
            pl.BlockSpec(memory_space=pl.ANY),
            pl.BlockSpec(memory_space=pl.ANY),
        ],
        out_specs=[
            pl.BlockSpec((some, PAIRS, BLK, 2 * BLK), lambda i: (jnp.maximum(i - count, 0), 0, 0, 0)),
            pl.BlockSpec((BEAMS, 2, 2 * SPEC, lanes), lambda i: (0, 0, 0, 0)),
        ],
        scratch_shapes=[
            pltpu.VMEM((2 * R1, 32, R2), F32),
            pltpu.VMEM((4, 16, SPEC, R2), F32),
            pltpu.VMEM((512, 256), BF16),
            pltpu.VMEM((512, 256), BF16),
            pltpu.VMEM((OUTCH * SEND_GROUP, R2), F32),
            pltpu.VMEM((devices, per_dest, parts, SEND_GROUP, R2), BF16),
            pltpu.VMEM((per_dest, devices * parts, SEND_GROUP, R2), BF16),
            pltpu.VMEM((stn,) + gain.shape, F32),
            pltpu.VMEM((stn,) + delay.shape, F32),
            pltpu.VMEM((per_dest, FAVG * BEAMS, STATIONS), BF16),
            pltpu.VMEM((per_dest, FAVG * BEAMS, STATIONS), BF16),
            pltpu.VMEM((some, NBLK, 2 * BLK, R2), BF16),
            pltpu.VMEM((some, INPUTS, R2), F32),
            pltpu.VMEM((per_dest * 2 * BEAMS, R2), F32),
            pltpu.SemaphoreType.DMA,
            pltpu.SemaphoreType.DMA,
            pltpu.SemaphoreType.DMA((chunks,)),
            pltpu.SemaphoreType.DMA,
            pltpu.SemaphoreType.DMA((2, stn)),
            pltpu.SemaphoreType.DMA((2, stn)),
            pltpu.SemaphoreType.DMA((2,)),
        ],
        compiler_params=pltpu.CompilerParams(
            vmem_limit_bytes=60 << 20, collective_id=0, has_side_effects=True
        ),
        name="station_beamformer",
    )(
        by_sample(voltages),
        filter_taps,
        jnp.asarray(tw),
        jnp.asarray(mtw),
        jnp.asarray(f2),
        block_pairs.T,
        stations,
        gain,
        delay,
    )
    return visibilities, jnp.swapaxes(beams, 2, 3)


def spectra_of_channels(voltages, filter_taps, gain, delay, stn, chan):
    count = voltages.shape[0]
    devices = stn * chan
    per_dest = OUTCH // devices
    spectra = channelize(voltages, filter_taps, devices)
    moved = lax.all_to_all(spectra, ("stn", "chan"), split_axis=0, concat_axis=0, tiled=True)
    turned = jnp.transpose(moved, (1, 0, 2, 3)).reshape(per_dest, devices * count, R2)
    gains = lax.all_gather(gain, "stn", axis=0, tiled=True)
    delays = lax.all_gather(delay, "stn", axis=0, tiled=True)
    return turned, gains, delays


def correlate_kernel(pairs, x_ref, wr_ref, wi_ref, vis_ref, beam_ref, both, wide, sums):
    chunk = pl.program_id(0)
    some = x_ref.shape[0]
    lane = lax.broadcasted_iota(jnp.int32, (1, R2), 1)
    sign = jnp.where(lane < 64, -1.0, 1.0).astype(F32)
    of = (lane // SPEC) % FAVG
    for o in range(some):
        for k in range(NBLK):
            x = x_ref[o, k * BLK : (k + 1) * BLK, :]
            xf = x.astype(F32)
            wide[o, k * BLK : (k + 1) * BLK, :] = xf
            both[o, k, 0:BLK, :] = x
            both[o, k, BLK : 2 * BLK, :] = (pltpu.roll(xf, 64, 1) * sign).astype(BF16)
        for r in range(PAIRS):
            rows = both[o, pairs[0, r], 0:BLK, :]
            vis = lax.dot_general(rows, both[o, pairs[1, r]], NT, preferred_element_type=F32)
            vis_ref[o, r] = (vis * (1.0 / (FAVG * SPEC))).astype(BF16)
        for p in range(2):
            x = wide.at[o][pl.ds(p, STATIONS, stride=2), :].astype(BF16)
            real = jnp.dot(wr_ref[o], x, preferred_element_type=F32)
            imag = jnp.dot(wi_ref[o], x, preferred_element_type=F32)
            beams = real + sign * pltpu.roll(imag, 64, 1)
            total = beams[0:BEAMS]
            for f in range(1, FAVG):
                total = jnp.where(of == f, beams[f * BEAMS : (f + 1) * BEAMS], total)
            first = pl.multiple_of(((chunk * some + o) * 2 + p) * BEAMS, BEAMS)
            sums[pl.ds(first, BEAMS), :] = total

    @pl.when(chunk == pl.num_programs(0) - 1)
    def _():
        turn_beams(sums, beam_ref)


def turn_beams(sums, beam_ref):
    lanes = beam_ref.shape[3]
    count = lanes // FAVG
    column = lax.broadcasted_iota(jnp.int32, (count, lanes), 1)
    spread = jnp.where(column // FAVG == lax.broadcasted_iota(jnp.int32, (count, lanes), 0), 1.0, 0.0)
    spread = spread.astype(BF16)
    fine = lax.broadcasted_iota(jnp.int32, (1, lanes), 1) % FAVG
    for p in range(2):
        for b in range(BEAMS):
            rows = sums[pl.ds(p * BEAMS + b, count, stride=2 * BEAMS), :].astype(BF16)
            moved = lax.dot_general(rows, spread, TN, preferred_element_type=F32)
            for q in range(2):
                total = moved[q * 64 : q * 64 + SPEC]
                for f in range(1, FAVG):
                    total = jnp.where(fine == f, moved[q * 64 + f * SPEC : q * 64 + (f + 1) * SPEC], total)
                beam_ref[b, p, q * SPEC : (q + 1) * SPEC, :] = total.astype(BF16)


def correlate(turned, real, imag, block_pairs):
    per_dest = turned.shape[0]
    lanes = FAVG * per_dest
    some = math.gcd(per_dest, 4)
    weight_spec = pl.BlockSpec((some, FAVG * BEAMS, STATIONS), lambda o, pairs: (o, 0, 0))
    visibilities, beams = pl.pallas_call(
        correlate_kernel,
        grid_spec=pltpu.PrefetchScalarGridSpec(
            num_scalar_prefetch=1,
            grid=(per_dest // some,),
            in_specs=[
                pl.BlockSpec((some, INPUTS, R2), lambda o, pairs: (o, 0, 0)),
                weight_spec,
                weight_spec,
            ],
            out_specs=[
                pl.BlockSpec((some, PAIRS, BLK, 2 * BLK), lambda o, pairs: (o, 0, 0, 0)),
                pl.BlockSpec((BEAMS, 2, 2 * SPEC, lanes), lambda o, pairs: (0, 0, 0, 0)),
            ],
            scratch_shapes=[
                pltpu.VMEM((some, NBLK, 2 * BLK, R2), BF16),
                pltpu.VMEM((some, INPUTS, R2), F32),
                pltpu.VMEM((per_dest * 2 * BEAMS, R2), F32),
            ],
        ),
        out_shape=[
            jax.ShapeDtypeStruct((per_dest, PAIRS, BLK, 2 * BLK), BF16),
            jax.ShapeDtypeStruct((BEAMS, 2, 2 * SPEC, lanes), BF16),
        ],
        name="correlate",
    )(block_pairs.T, turned, real, imag)
    return visibilities, jnp.swapaxes(beams, 2, 3)


def beam_weights(stations, gains, delays, chan_start, per_dest):
    named = stations[:, :, None] == jnp.arange(STATIONS, dtype=jnp.int32)[None, None, :]
    gain = jnp.sum(jnp.where(named, gains[:, :, None] / math.sqrt(LIST), 0.0), axis=1)
    delay = jnp.sum(jnp.where(named, delays[:, :, None], 0.0), axis=1)
    rate = 2.0 * math.pi / NFFT * delay
    coarse = (chan_start + FAVG * jnp.arange(per_dest, dtype=jnp.int32)).astype(F32)
    base = rate[None] * coarse[:, None, None]
    base_cos, base_sin = gain * jnp.cos(base), gain * jnp.sin(base)
    fine = rate[None] * jnp.arange(FAVG, dtype=jnp.int32).astype(F32)[:, None, None]
    fine_cos, fine_sin = jnp.cos(fine)[None], jnp.sin(fine)[None]
    base_cos, base_sin = base_cos[:, None], base_sin[:, None]
    real = base_cos * fine_cos - base_sin * fine_sin
    imag = -(base_sin * fine_cos + base_cos * fine_sin)
    shape = (per_dest, FAVG * BEAMS, STATIONS)
    return real.astype(BF16).reshape(shape), imag.astype(BF16).reshape(shape)


def shards(voltages, filter_taps, beam_stations, beam_gain, beam_delay, block_pairs):
    stn = lax.axis_size("stn")
    chan = lax.axis_size("chan")
    devices = stn * chan
    per_dest = OUTCH // devices
    chan_start = (lax.axis_index("stn") * chan + lax.axis_index("chan")) * (NFFT // devices)
    if voltages.shape[0] % SEND_GROUP == 0 and voltages.shape[0] > LATE and per_dest % CHUNK == 0:
        return fused(
            voltages, filter_taps, beam_stations, beam_gain, beam_delay, block_pairs, stn, chan
        )
    turned, gains, delays = spectra_of_channels(
        voltages, filter_taps, beam_gain, beam_delay, stn, chan
    )
    real, imag = beam_weights(beam_stations, gains, delays, chan_start, per_dest)
    return correlate(turned, real, imag, block_pairs)


def solution(mesh):
    placed = (P(("stn", "chan"), None, None, None), P(), P(), P("stn", None), P("stn", None), P())
    return jax.shard_map(
        shards,
        mesh=mesh,
        in_specs=placed,
        out_specs=(P(("stn", "chan"), None, None, None), P(None, None, ("stn", "chan"), None)),
        check_vma=False,
    )
```

```python
import functools
import math

import jax
import jax.numpy as jnp
import numpy as np
from jax import lax
from jax.experimental import pallas as pl
from jax.experimental.pallas import tpu as pltpu
from jax.sharding import PartitionSpec as P

STATIONS = 512
INPUTS = 1024
NFFT = 4096
BEAMS = 16
TAPS = 12
FAVG = 4
BLK = 64
LIST = 128
SPEC = 16
FRAMES = 27
NBLK = 16
PAIRS = 16
R1 = 32
R2 = 128
GROUPS = R1 // FAVG
OUTCH = NFFT // FAVG
SEND_GROUP = 2
LATE = 16
CHUNK = 2
F32 = jnp.float32
BF16 = jnp.bfloat16
NT = (((1,), (1,)), ((), ()))
TN = (((0,), (0,)), ((), ()))


def tables():
    b = np.arange(R2)
    ang = 2.0 * np.pi * (b[:, None] * b[None, :] % R2) / R2
    f2 = np.block([[np.cos(ang), np.sin(ang)], [-np.sin(ang), np.cos(ang)]])
    hi = f2.astype(jnp.bfloat16)
    lo = (f2 - hi.astype(np.float64)).astype(jnp.bfloat16)
    f2 = np.concatenate([hi, lo], axis=0)
    ang = 2.0 * np.pi * (np.arange(R1)[:, None] * b[None, :]) / NFFT
    tw = np.stack([np.cos(ang), -np.sin(ang)], axis=1) / math.sqrt(NFFT)
    ang = 2.0 * np.pi * (np.arange(8)[:, None] * np.arange(4)[None, :]) / R1
    mid = np.stack([np.cos(ang), -np.sin(ang)], axis=-1).reshape(8, 8, 1)
    mid = np.broadcast_to(mid, (8, 8, R2))
    return f2, tw.astype(np.float32), mid.astype(np.float32)


def add(x, y):
    return (x[0] + y[0], x[1] + y[1])


def sub(x, y):
    return (x[0] - y[0], x[1] - y[1])


def turn(x):
    return (x[1], -x[0])


def dft4(x):
    p, m = add(x[0], x[2]), sub(x[0], x[2])
    q, n = add(x[1], x[3]), turn(sub(x[1], x[3]))
    return [add(p, q), add(m, n), sub(p, q), sub(m, n)]


def dft8(x):
    even = dft4(x[0::2])
    odd = dft4(x[1::2])
    h = math.sqrt(0.5)
    o1, o3 = odd[1], odd[3]
    odd = [
        odd[0],
        ((o1[0] + o1[1]) * h, (o1[1] - o1[0]) * h),
        turn(odd[2]),
        ((o3[1] - o3[0]) * h, -(o3[0] + o3[1]) * h),
    ]
    return [add(e, o) for e, o in zip(even, odd)] + [sub(e, o) for e, o in zip(even, odd)]


def transform(group, step, v_ref, taps_ref, tw_ref, mtw_ref, f2_ref, vs, mid, y_hi, y_lo, os):
    rows = vs.reshape(2 * R1 * 32, R2)
    for frame in range(FRAMES):
        rows[pl.ds(frame, 2 * R1, stride=32), :] = v_ref[frame].astype(F32)

    def low(a_lo, carry):
        x = []
        for a_hi in range(4):
            a = a_lo + 8 * a_hi
            parts = [None, None]
            for t in range(TAPS):
                tap = taps_ref[t : t + 1, pl.ds(pl.multiple_of(a * R2, R2), R2)]
                for q in range(2):
                    term = tap * vs[2 * a + q, t : t + SPEC, :]
                    parts[q] = term if t == 0 else parts[q] + term
            x.append(tuple(parts))
        z = dft4(x)
        for k in range(4):
            zr, zi = z[k]
            if k:
                wr = mtw_ref[a_lo, 2 * k : 2 * k + 1, :]
                wi = mtw_ref[a_lo, 2 * k + 1 : 2 * k + 2, :]
                zr, zi = zr * wr - zi * wi, zr * wi + zi * wr
            mid[k, 2 * a_lo] = zr
            mid[k, 2 * a_lo + 1] = zi
        return carry

    lax.fori_loop(0, 8, low, 0)
    for k in range(4):
        z = dft8([(mid[k, 2 * a], mid[k, 2 * a + 1]) for a in range(8)])
        for k2 in range(8):
            c1 = k + 4 * k2
            zr, zi = z[k2]
            wr, wi = tw_ref[c1, 0:1, :], tw_ref[c1, 1:2, :]
            for q, val in enumerate((zr * wr - zi * wi, zr * wi + zi * wr)):
                hi = val.astype(BF16)
                y_hi[c1 * SPEC : (c1 + 1) * SPEC, q * R2 : (q + 1) * R2] = hi
                y_lo[c1 * SPEC : (c1 + 1) * SPEC, q * R2 : (q + 1) * R2] = (
                    val - hi.astype(F32)
                ).astype(BF16)
    left = lax.broadcasted_iota(jnp.int32, (R2, R2), 1) < 64
    for h in range(2):
        yh = y_hi[h * 256 : (h + 1) * 256, :]
        yl = y_lo[h * 256 : (h + 1) * 256, :]
        full = lax.dot_general(f2_ref[...], yh, NT, preferred_element_type=F32)
        res = full[0:256] + full[256:512]
        res = res + lax.dot_general(f2_ref[0:256, :], yl, NT, preferred_element_type=F32)
        for j in range(2):
            re = res[0:R2, j * R2 : (j + 1) * R2]
            im = res[R2 : 2 * R2, j * R2 : (j + 1) * R2]
            first = jnp.where(left, re, pltpu.roll(im, 64, 1))
            second = jnp.where(left, pltpu.roll(re, 64, 1), im)
            g = 4 * h + 2 * j
            os[pl.ds(g * group + step, R2, stride=GROUPS * group), :] = first
            os[pl.ds((g + 1) * group + step, R2, stride=GROUPS * group), :] = second


def fft_kernel(group, v_ref, taps_ref, tw_ref, mtw_ref, f2_ref, out_ref, vs, mid, y_hi, y_lo, os):
    step = pl.program_id(1)
    transform(group, step, v_ref, taps_ref, tw_ref, mtw_ref, f2_ref, vs, mid, y_hi, y_lo, os)

    @pl.when(step == group - 1)
    def _():
        n_dest, per_dest = out_ref.shape[0], out_ref.shape[1]

        def emit(dest, carry):
            size = per_dest * group
            part = os[pl.ds(pl.multiple_of(dest * size, size), size), :]
            out_ref[dest] = part.reshape(per_dest, group, R2).astype(BF16)
            return carry

        lax.fori_loop(0, n_dest, emit, 0)


def by_sample(voltages):
    count = voltages.shape[0]
    split = voltages.reshape(count, FRAMES, 2, R1, R2)
    return jnp.transpose(split, (0, 1, 3, 2, 4)).reshape(count, FRAMES, 2 * R1, R2)


def channelize(voltages, filter_taps, devices):
    count = voltages.shape[0]
    group = min(16, count)
    per_dest = OUTCH // devices
    f2, tw, mtw = tables()
    return pl.pallas_call(
        functools.partial(fft_kernel, group),
        grid=(count // group, group),
        out_shape=jax.ShapeDtypeStruct((devices, per_dest, count, R2), BF16),
        in_specs=[
            pl.BlockSpec((None, FRAMES, 2 * R1, R2), lambda i, j: (i * group + j, 0, 0, 0)),
            pl.BlockSpec((TAPS, NFFT), lambda i, j: (0, 0)),
            pl.BlockSpec((R1, 2, R2), lambda i, j: (0, 0, 0)),
            pl.BlockSpec((8, 8, R2), lambda i, j: (0, 0, 0)),
            pl.BlockSpec((512, 256), lambda i, j: (0, 0)),
        ],
        out_specs=pl.BlockSpec((devices, per_dest, group, R2), lambda i, j: (0, 0, i, 0)),
        scratch_shapes=[
            pltpu.VMEM((2 * R1, 32, R2), F32),
            pltpu.VMEM((4, 16, SPEC, R2), F32),
            pltpu.VMEM((512, 256), BF16),
            pltpu.VMEM((512, 256), BF16),
            pltpu.VMEM((OUTCH * group, R2), F32),
        ],
        compiler_params=pltpu.CompilerParams(vmem_limit_bytes=48 << 20),
        name="channelize",
    )(
        by_sample(voltages),
        filter_taps,
        jnp.asarray(tw),
        jnp.asarray(mtw),
        jnp.asarray(f2),
    )


def steer(first_channel, stations, gains, delays, wr, wi):
    highest = lax.Precision.HIGHEST
    table = jnp.concatenate([gains / math.sqrt(LIST), delays * (2.0 * math.pi / NFFT)], axis=0)
    beam = lax.broadcasted_iota(jnp.int32, (2 * BEAMS, 1), 0) % BEAMS
    spread = jnp.zeros((2 * BEAMS, STATIONS), F32)
    for b in range(BEAMS):
        named = lax.broadcasted_iota(jnp.int32, (STATIONS, LIST), 0) == stations[b : b + 1, :]
        row = jnp.where(beam == b, table, 0.0)
        spread += lax.dot_general(
            row, named.astype(F32), NT, precision=highest, preferred_element_type=F32
        )
    gain, rate = spread[0:BEAMS], spread[BEAMS:]
    fine = [(jnp.cos(rate * float(f)), jnp.sin(rate * float(f))) for f in range(FAVG)]

    def one(o, carry):
        base = rate * (first_channel + FAVG * o).astype(F32)
        base_cos, base_sin = gain * jnp.cos(base), gain * jnp.sin(base)
        for f, (fine_cos, fine_sin) in enumerate(fine):
            real = base_cos * fine_cos - base_sin * fine_sin
            imag = -(base_sin * fine_cos + base_cos * fine_sin)
            wr[o, f * BEAMS : (f + 1) * BEAMS, :] = real.astype(BF16)
            wi[o, f * BEAMS : (f + 1) * BEAMS, :] = imag.astype(BF16)
        return carry

    lax.fori_loop(0, wr.shape[0], one, 0)


def station_kernel(
    stn, chan, v_ref, taps_ref, tw_ref, mtw_ref, f2_ref, pairs, stations, gain, delay, vis, last, wr, wi, sums,
    vs, mid, y_hi, y_lo, os, stage, x, gains, delays, both, wide,
    send_sem, early_sem, late_sem, own_sem, beam_send, beam_recv, beam_own,
):
    devices = stn * chan
    row, column = lax.axis_index("stn"), lax.axis_index("chan")
    me = row * chan + column
    now = pl.program_id(0)
    per_dest, parts = stage.shape[1], stage.shape[2]
    count = parts * SEND_GROUP
    late = LATE // SEND_GROUP
    early = parts - late
    some = CHUNK
    chunks = per_dest // some
    part, step = now // SEND_GROUP, now % SEND_GROUP
    barrier = pltpu.get_barrier_semaphore()
    small = ((gain, gains), (delay, delays))

    def peer(k):
        dest = lax.rem(me + k, devices)
        return dest, (dest // chan, lax.rem(dest, chan))

    def beam_copy(which, k):
        return pltpu.make_async_remote_copy(
            src_ref=small[which][0],
            dst_ref=small[which][1].at[row],
            send_sem=beam_send.at[which, k],
            recv_sem=beam_recv.at[which, k],
            device_id=(lax.rem(row + k, stn), column),
            device_id_type=pl.DeviceIdType.MESH,
        )

    def beam_keep(which):
        return pltpu.make_async_copy(small[which][0], small[which][1].at[row], beam_own.at[which])

    def copy(k, outs, first, size, sem):
        dest, where = peer(k)
        return pltpu.make_async_remote_copy(
            src_ref=stage.at[dest, outs, pl.ds(first, size)],
            dst_ref=x.at[outs, pl.ds(me * parts + first, size)],
            send_sem=send_sem,
            recv_sem=sem,
            device_id=where,
            device_id_type=pl.DeviceIdType.MESH,
        )

    def own():
        return pltpu.make_async_copy(stage.at[me], x.at[:, pl.ds(me * parts, parts)], own_sem)

    def arrived(outs, size, sem):
        ref = x.at[outs, pl.ds(0, (devices - 1) * size)]
        pltpu.make_async_copy(ref, ref, sem).wait()

    def rows_of(out, k):
        return x[out, pl.ds(k * (BLK // SEND_GROUP), BLK // SEND_GROUP)].reshape(BLK, R2)

    def fill(dest):
        size = per_dest * SEND_GROUP
        rows = os[pl.ds(pl.multiple_of(dest * size, size), size), :]
        stage[dest, :, pl.ds(part, 1)] = rows.reshape(per_dest, 1, SEND_GROUP, R2).astype(BF16)

    @pl.when(now == 0)
    def _():
        def greet(k, carry):
            pl.semaphore_signal(
                barrier, inc=1, device_id=peer(k)[1], device_id_type=pl.DeviceIdType.MESH
            )
            return carry

        lax.fori_loop(1, devices, greet, 0)

    @pl.when(now < count)
    def _():
        transform(SEND_GROUP, step, v_ref, taps_ref, tw_ref, mtw_ref, f2_ref, vs, mid, y_hi, y_lo, os)

    @pl.when(now == SEND_GROUP - 1)
    def _():
        pl.semaphore_wait(barrier, devices - 1)
        for which in range(2):
            for k in range(1, stn):
                beam_copy(which, k).start()
            beam_keep(which).start()

    @pl.when((now < count) & (step == SEND_GROUP - 1) & (part < early))
    def _():
        def emit(k, carry):
            fill(peer(k)[0])
            copy(k, slice(None), part, 1, early_sem).start()
            return carry

        lax.fori_loop(1, devices, emit, 0)
        fill(me)

    @pl.when((now < count) & (step == SEND_GROUP - 1) & (part >= early))
    def _():
        def emit(dest, carry):
            fill(dest)
            return carry

        lax.fori_loop(0, devices, emit, 0)

    @pl.when(now == count - 1)
    def _():
        def emit(n, carry):
            chunk, k = n // (devices - 1), 1 + lax.rem(n, devices - 1)
            copy(k, pl.ds(chunk * some, some), early, late, late_sem.at[chunk]).start()
            return carry

        lax.fori_loop(0, chunks * (devices - 1), emit, 0)
        own().start()
        for which in range(2):
            for k in range(1, stn):
                beam_copy(which, k).wait()
            beam_keep(which).wait()
        every = [jnp.concatenate([ref[r] for r in range(stn)], axis=0) for ref in (gains, delays)]
        steer(me * (per_dest * FAVG), stations[...], every[0], every[1], wr, wi)
        own().wait()
        arrived(slice(None), early, early_sem)

    @pl.when(now >= count)
    def _():
        chunk = now - count
        arrived(pl.ds(chunk * some, some), late, late_sem.at[chunk])

        @pl.when(chunk < chunks - 1)
        def _():
            correlate_chunk(chunk, chunk, pairs, rows_of, wr, wi, vis, both, wide, sums)

    @pl.when(now == count + chunks - 1)
    def _():
        def keep(n, carry):
            o, k = n // NBLK, lax.rem(n, NBLK)
            last[o, pl.ds(pl.multiple_of(k * BLK, BLK), BLK), :] = rows_of((chunks - 1) * some + o, k)
            return carry

        lax.fori_loop(0, some * NBLK, keep, 0)
        sent = stage.at[pl.ds(0, devices - 1)]
        pltpu.make_async_copy(sent, sent, send_sem).wait()


def correlate_chunk(chunk, slot, pairs, rows_of, wr_ref, wi_ref, vis_ref, both, wide, sums):
    some = CHUNK
    lane = lax.broadcasted_iota(jnp.int32, (1, R2), 1)
    sign = jnp.where(lane < 64, -1.0, 1.0).astype(F32)
    of = (lane // SPEC) % FAVG

    def one(o, carry):
        out = chunk * some + o
        for k in range(NBLK):
            x = rows_of(out, k)
            xf = x.astype(F32)
            wide[o, k * BLK : (k + 1) * BLK, :] = xf
            both[o, k, 0:BLK, :] = x
            both[o, k, BLK : 2 * BLK, :] = (pltpu.roll(xf, 64, 1) * sign).astype(BF16)
        for r in range(PAIRS):
            rows = both[o, pairs[0, r], 0:BLK, :]
            vis = lax.dot_general(rows, both[o, pairs[1, r]], NT, preferred_element_type=F32)
            vis_ref[slot * some + o, r] = (vis * (1.0 / (FAVG * SPEC))).astype(BF16)
        for p in range(2):
            x = wide.at[o][pl.ds(p, STATIONS, stride=2), :].astype(BF16)
            real = jnp.dot(wr_ref[out], x, preferred_element_type=F32)
            imag = jnp.dot(wi_ref[out], x, preferred_element_type=F32)
            beams = real + sign * pltpu.roll(imag, 64, 1)
            total = beams[0:BEAMS]
            for f in range(1, FAVG):
                total = jnp.where(of == f, beams[f * BEAMS : (f + 1) * BEAMS], total)
            first = pl.multiple_of((out * 2 + p) * BEAMS, BEAMS)
            sums[pl.ds(first, BEAMS), :] = total
        return carry

    lax.fori_loop(0, some, one, 0)


def finish_kernel(pairs, part_ref, x_ref, wr_ref, wi_ref, sums_ref, vis_ref, beam_ref, last, both, wide, sums, sem):
    some = CHUNK
    chunks = vis_ref.shape[0] // some
    first = (chunks - 1) * some

    def rows_of(out, k):
        return x_ref[out - first, k * BLK : (k + 1) * BLK, :]

    held = sums_ref.shape[0] - some * 2 * BEAMS

    def copy(chunk, src):
        return pltpu.make_async_copy(src, vis_ref.at[pl.ds(chunk * some, some)], sem.at[chunk])

    for chunk in range(chunks - 1):
        copy(chunk, part_ref.at[pl.ds(chunk * some, some)]).start()
    correlate_chunk(chunks - 1, 0, pairs, rows_of, wr_ref, wi_ref, last, both, wide, sums)
    copy(chunks - 1, last).start()
    sums[0:held, :] = sums_ref[0:held, :]
    turn_beams(sums, beam_ref)
    for chunk in range(chunks - 1):
        copy(chunk, part_ref.at[pl.ds(chunk * some, some)]).wait()
    copy(chunks - 1, last).wait()


def fused(voltages, filter_taps, stations, gain, delay, block_pairs, stn, chan):
    count = voltages.shape[0]
    devices = stn * chan
    per_dest = OUTCH // devices
    parts = count // SEND_GROUP
    some = CHUNK
    chunks = per_dest // some
    lanes = FAVG * per_dest
    f2, tw, mtw = tables()
    held = [
        pltpu.VMEM((per_dest, PAIRS, BLK, 2 * BLK), BF16),
        pltpu.VMEM((some, INPUTS, R2), BF16),
        pltpu.VMEM((per_dest, FAVG * BEAMS, STATIONS), BF16),
        pltpu.VMEM((per_dest, FAVG * BEAMS, STATIONS), BF16),
        pltpu.VMEM((per_dest * 2 * BEAMS, R2), F32),
    ]
    worked = pl.pallas_call(
        functools.partial(station_kernel, stn, chan),
        grid=(count + chunks,),
        out_shape=held,
        in_specs=[
            pl.BlockSpec((None, FRAMES, 2 * R1, R2), lambda i: (jnp.minimum(i, count - 1), 0, 0, 0)),
            pl.BlockSpec((TAPS, NFFT), lambda i: (0, 0)),
            pl.BlockSpec((R1, 2, R2), lambda i: (0, 0, 0)),
            pl.BlockSpec((8, 8, R2), lambda i: (0, 0, 0)),
            pl.BlockSpec((512, 256), lambda i: (0, 0)),
            pl.BlockSpec(memory_space=pltpu.SMEM),
            pl.BlockSpec((BEAMS, LIST), lambda i: (0, 0)),
            pl.BlockSpec(memory_space=pl.ANY),
            pl.BlockSpec(memory_space=pl.ANY),
        ],
        out_specs=[pl.BlockSpec(memory_space=pltpu.VMEM)] * len(held),
        scratch_shapes=[
            pltpu.VMEM((2 * R1, 32, R2), F32),
            pltpu.VMEM((4, 16, SPEC, R2), F32),
            pltpu.VMEM((512, 256), BF16),
            pltpu.VMEM((512, 256), BF16),
            pltpu.VMEM((OUTCH * SEND_GROUP, R2), F32),
            pltpu.VMEM((devices, per_dest, parts, SEND_GROUP, R2), BF16),
            pltpu.VMEM((per_dest, devices * parts, SEND_GROUP, R2), BF16),
            pltpu.VMEM((stn,) + gain.shape, F32),
            pltpu.VMEM((stn,) + delay.shape, F32),
            pltpu.VMEM((some, NBLK, 2 * BLK, R2), BF16),
            pltpu.VMEM((some, INPUTS, R2), F32),
            pltpu.SemaphoreType.DMA,
            pltpu.SemaphoreType.DMA,
            pltpu.SemaphoreType.DMA((chunks,)),
            pltpu.SemaphoreType.DMA,
            pltpu.SemaphoreType.DMA((2, stn)),
            pltpu.SemaphoreType.DMA((2, stn)),
            pltpu.SemaphoreType.DMA((2,)),
        ],
        compiler_params=pltpu.CompilerParams(
            vmem_limit_bytes=48 << 20, collective_id=0, has_side_effects=True
        ),
        name="station_beamformer",
    )(
        by_sample(voltages),
        filter_taps,
        jnp.asarray(tw),
        jnp.asarray(mtw),
        jnp.asarray(f2),
        block_pairs.T,
        stations,
        gain,
        delay,
    )
    whole = pl.BlockSpec(memory_space=pltpu.VMEM)
    visibilities, beams = pl.pallas_call(
        finish_kernel,
        out_shape=[
            jax.ShapeDtypeStruct((per_dest, PAIRS, BLK, 2 * BLK), BF16),
            jax.ShapeDtypeStruct((BEAMS, 2, 2 * SPEC, lanes), BF16),
        ],
        in_specs=[pl.BlockSpec(memory_space=pltpu.SMEM)] + [whole] * len(held),
        out_specs=[pl.BlockSpec(memory_space=pl.ANY), whole],
        scratch_shapes=[
            pltpu.VMEM((some, PAIRS, BLK, 2 * BLK), BF16),
            pltpu.VMEM((some, NBLK, 2 * BLK, R2), BF16),
            pltpu.VMEM((some, INPUTS, R2), F32),
            pltpu.VMEM((per_dest * 2 * BEAMS, R2), F32),
            pltpu.SemaphoreType.DMA((chunks,)),
        ],
        compiler_params=pltpu.CompilerParams(vmem_limit_bytes=16 << 20),
        name="finish",
    )(block_pairs.T, *worked)
    return visibilities, jnp.swapaxes(beams, 2, 3)


def spectra_of_channels(voltages, filter_taps, gain, delay, stn, chan):
    count = voltages.shape[0]
    devices = stn * chan
    per_dest = OUTCH // devices
    spectra = channelize(voltages, filter_taps, devices)
    moved = lax.all_to_all(spectra, ("stn", "chan"), split_axis=0, concat_axis=0, tiled=True)
    turned = jnp.transpose(moved, (1, 0, 2, 3)).reshape(per_dest, devices * count, R2)
    gains = lax.all_gather(gain, "stn", axis=0, tiled=True)
    delays = lax.all_gather(delay, "stn", axis=0, tiled=True)
    return turned, gains, delays


def correlate_kernel(pairs, x_ref, wr_ref, wi_ref, vis_ref, beam_ref, both, wide, sums):
    chunk = pl.program_id(0)
    some = x_ref.shape[0]
    lane = lax.broadcasted_iota(jnp.int32, (1, R2), 1)
    sign = jnp.where(lane < 64, -1.0, 1.0).astype(F32)
    of = (lane // SPEC) % FAVG
    for o in range(some):
        for k in range(NBLK):
            x = x_ref[o, k * BLK : (k + 1) * BLK, :]
            xf = x.astype(F32)
            wide[o, k * BLK : (k + 1) * BLK, :] = xf
            both[o, k, 0:BLK, :] = x
            both[o, k, BLK : 2 * BLK, :] = (pltpu.roll(xf, 64, 1) * sign).astype(BF16)
        for r in range(PAIRS):
            rows = both[o, pairs[0, r], 0:BLK, :]
            vis = lax.dot_general(rows, both[o, pairs[1, r]], NT, preferred_element_type=F32)
            vis_ref[o, r] = (vis * (1.0 / (FAVG * SPEC))).astype(BF16)
        for p in range(2):
            x = wide.at[o][pl.ds(p, STATIONS, stride=2), :].astype(BF16)
            real = jnp.dot(wr_ref[o], x, preferred_element_type=F32)
            imag = jnp.dot(wi_ref[o], x, preferred_element_type=F32)
            beams = real + sign * pltpu.roll(imag, 64, 1)
            total = beams[0:BEAMS]
            for f in range(1, FAVG):
                total = jnp.where(of == f, beams[f * BEAMS : (f + 1) * BEAMS], total)
            first = pl.multiple_of(((chunk * some + o) * 2 + p) * BEAMS, BEAMS)
            sums[pl.ds(first, BEAMS), :] = total

    @pl.when(chunk == pl.num_programs(0) - 1)
    def _():
        turn_beams(sums, beam_ref)


def turn_beams(sums, beam_ref):
    lanes = beam_ref.shape[3]
    count = lanes // FAVG
    column = lax.broadcasted_iota(jnp.int32, (count, lanes), 1)
    spread = jnp.where(column // FAVG == lax.broadcasted_iota(jnp.int32, (count, lanes), 0), 1.0, 0.0)
    spread = spread.astype(BF16)
    fine = lax.broadcasted_iota(jnp.int32, (1, lanes), 1) % FAVG
    for p in range(2):
        for b in range(BEAMS):
            rows = sums[pl.ds(p * BEAMS + b, count, stride=2 * BEAMS), :].astype(BF16)
            moved = lax.dot_general(rows, spread, TN, preferred_element_type=F32)
            for q in range(2):
                total = moved[q * 64 : q * 64 + SPEC]
                for f in range(1, FAVG):
                    total = jnp.where(fine == f, moved[q * 64 + f * SPEC : q * 64 + (f + 1) * SPEC], total)
                beam_ref[b, p, q * SPEC : (q + 1) * SPEC, :] = total.astype(BF16)


def correlate(turned, real, imag, block_pairs):
    per_dest = turned.shape[0]
    lanes = FAVG * per_dest
    some = math.gcd(per_dest, 4)
    weight_spec = pl.BlockSpec((some, FAVG * BEAMS, STATIONS), lambda o, pairs: (o, 0, 0))
    visibilities, beams = pl.pallas_call(
        correlate_kernel,
        grid_spec=pltpu.PrefetchScalarGridSpec(
            num_scalar_prefetch=1,
            grid=(per_dest // some,),
            in_specs=[
                pl.BlockSpec((some, INPUTS, R2), lambda o, pairs: (o, 0, 0)),
                weight_spec,
                weight_spec,
            ],
            out_specs=[
                pl.BlockSpec((some, PAIRS, BLK, 2 * BLK), lambda o, pairs: (o, 0, 0, 0)),
                pl.BlockSpec((BEAMS, 2, 2 * SPEC, lanes), lambda o, pairs: (0, 0, 0, 0)),
            ],
            scratch_shapes=[
                pltpu.VMEM((some, NBLK, 2 * BLK, R2), BF16),
                pltpu.VMEM((some, INPUTS, R2), F32),
                pltpu.VMEM((per_dest * 2 * BEAMS, R2), F32),
            ],
        ),
        out_shape=[
            jax.ShapeDtypeStruct((per_dest, PAIRS, BLK, 2 * BLK), BF16),
            jax.ShapeDtypeStruct((BEAMS, 2, 2 * SPEC, lanes), BF16),
        ],
        name="correlate",
    )(block_pairs.T, turned, real, imag)
    return visibilities, jnp.swapaxes(beams, 2, 3)


def beam_weights(stations, gains, delays, chan_start, per_dest):
    named = stations[:, :, None] == jnp.arange(STATIONS, dtype=jnp.int32)[None, None, :]
    gain = jnp.sum(jnp.where(named, gains[:, :, None] / math.sqrt(LIST), 0.0), axis=1)
    delay = jnp.sum(jnp.where(named, delays[:, :, None], 0.0), axis=1)
    rate = 2.0 * math.pi / NFFT * delay
    coarse = (chan_start + FAVG * jnp.arange(per_dest, dtype=jnp.int32)).astype(F32)
    base = rate[None] * coarse[:, None, None]
    base_cos, base_sin = gain * jnp.cos(base), gain * jnp.sin(base)
    fine = rate[None] * jnp.arange(FAVG, dtype=jnp.int32).astype(F32)[:, None, None]
    fine_cos, fine_sin = jnp.cos(fine)[None], jnp.sin(fine)[None]
    base_cos, base_sin = base_cos[:, None], base_sin[:, None]
    real = base_cos * fine_cos - base_sin * fine_sin
    imag = -(base_sin * fine_cos + base_cos * fine_sin)
    shape = (per_dest, FAVG * BEAMS, STATIONS)
    return real.astype(BF16).reshape(shape), imag.astype(BF16).reshape(shape)


def shards(voltages, filter_taps, beam_stations, beam_gain, beam_delay, block_pairs):
    stn = lax.axis_size("stn")
    chan = lax.axis_size("chan")
    devices = stn * chan
    per_dest = OUTCH // devices
    chan_start = (lax.axis_index("stn") * chan + lax.axis_index("chan")) * (NFFT // devices)
    if voltages.shape[0] % SEND_GROUP == 0 and voltages.shape[0] > LATE and per_dest % CHUNK == 0:
        return fused(
            voltages, filter_taps, beam_stations, beam_gain, beam_delay, block_pairs, stn, chan
        )
    turned, gains, delays = spectra_of_channels(
        voltages, filter_taps, beam_gain, beam_delay, stn, chan
    )
    real, imag = beam_weights(beam_stations, gains, delays, chan_start, per_dest)
    return correlate(turned, real, imag, block_pairs)


def solution(mesh):
    placed = (P(("stn", "chan"), None, None, None), P(), P(), P("stn", None), P("stn", None), P())
    return jax.shard_map(
        shards,
        mesh=mesh,
        in_specs=placed,
        out_specs=(P(("stn", "chan"), None, None, None), P(None, None, ("stn", "chan"), None)),
        check_vma=False,
    )
```

```python
import functools
import math

import jax
import jax.numpy as jnp
import numpy as np
from jax import lax
from jax.experimental import pallas as pl
from jax.experimental.pallas import tpu as pltpu
from jax.sharding import PartitionSpec as P

STATIONS = 512
INPUTS = 1024
NFFT = 4096
BEAMS = 16
TAPS = 12
FAVG = 4
BLK = 64
LIST = 128
SPEC = 16
FRAMES = 27
NBLK = 16
PAIRS = 16
R1 = 32
R2 = 128
GROUPS = R1 // FAVG
OUTCH = NFFT // FAVG
SEND_GROUP = 2
LATE = 16
CHUNK = 2
ROWS = 40
F32 = jnp.float32
BF16 = jnp.bfloat16
NT = (((1,), (1,)), ((), ()))
TN = (((0,), (0,)), ((), ()))


def tables():
    b = np.arange(R2)
    ang = 2.0 * np.pi * (b[:, None] * b[None, :] % R2) / R2
    f2 = np.block([[np.cos(ang), np.sin(ang)], [-np.sin(ang), np.cos(ang)]])
    hi = f2.astype(jnp.bfloat16)
    lo = (f2 - hi.astype(np.float64)).astype(jnp.bfloat16)
    f2 = np.concatenate([hi, lo], axis=0)
    ang = 2.0 * np.pi * (np.arange(R1)[:, None] * b[None, :]) / NFFT
    tw = np.stack([np.cos(ang), -np.sin(ang)], axis=1) / math.sqrt(NFFT)
    ang = 2.0 * np.pi * (np.arange(8)[:, None] * np.arange(4)[None, :]) / R1
    mid = np.stack([np.cos(ang), -np.sin(ang)], axis=-1).reshape(8, 8, 1)
    mid = np.broadcast_to(mid, (8, 8, R2))
    return f2, tw.astype(np.float32), mid.astype(np.float32)


def add(x, y):
    return (x[0] + y[0], x[1] + y[1])


def sub(x, y):
    return (x[0] - y[0], x[1] - y[1])


def turn(x):
    return (x[1], -x[0])


def dft4(x):
    p, m = add(x[0], x[2]), sub(x[0], x[2])
    q, n = add(x[1], x[3]), turn(sub(x[1], x[3]))
    return [add(p, q), add(m, n), sub(p, q), sub(m, n)]


def dft8(x):
    even = dft4(x[0::2])
    odd = dft4(x[1::2])
    h = math.sqrt(0.5)
    o1, o3 = odd[1], odd[3]
    odd = [
        odd[0],
        ((o1[0] + o1[1]) * h, (o1[1] - o1[0]) * h),
        turn(odd[2]),
        ((o3[1] - o3[0]) * h, -(o3[0] + o3[1]) * h),
    ]
    return [add(e, o) for e, o in zip(even, odd)] + [sub(e, o) for e, o in zip(even, odd)]


def transform(group, step, v_ref, taps_ref, tw_ref, mtw_ref, f2_ref, vs, mid, y_hi, y_lo, os):
    rows = vs.reshape(2 * R1 * ROWS, R2)
    for frame in range(FRAMES):
        rows[pl.ds(frame, 2 * R1, stride=ROWS), :] = v_ref[frame].astype(F32)

    def low(a_lo, carry):
        x = []
        for a_hi in range(4):
            a = a_lo + 8 * a_hi
            parts = [None, None]
            for t in range(TAPS):
                tap = taps_ref[t : t + 1, pl.ds(pl.multiple_of(a * R2, R2), R2)]
                for q in range(2):
                    term = tap * vs[2 * a + q, t : t + SPEC, :]
                    parts[q] = term if t == 0 else parts[q] + term
            x.append(tuple(parts))
        z = dft4(x)
        for k in range(4):
            zr, zi = z[k]
            if k:
                wr = mtw_ref[a_lo, 2 * k : 2 * k + 1, :]
                wi = mtw_ref[a_lo, 2 * k + 1 : 2 * k + 2, :]
                zr, zi = zr * wr - zi * wi, zr * wi + zi * wr
            mid[k, 2 * a_lo] = zr
            mid[k, 2 * a_lo + 1] = zi
        return carry

    lax.fori_loop(0, 8, low, 0)
    for k in range(4):
        z = dft8([(mid[k, 2 * a], mid[k, 2 * a + 1]) for a in range(8)])
        for k2 in range(8):
            c1 = k + 4 * k2
            zr, zi = z[k2]
            wr, wi = tw_ref[c1, 0:1, :], tw_ref[c1, 1:2, :]
            for q, val in enumerate((zr * wr - zi * wi, zr * wi + zi * wr)):
                hi = val.astype(BF16)
                y_hi[c1 * SPEC : (c1 + 1) * SPEC, q * R2 : (q + 1) * R2] = hi
                y_lo[c1 * SPEC : (c1 + 1) * SPEC, q * R2 : (q + 1) * R2] = (
                    val - hi.astype(F32)
                ).astype(BF16)
    left = lax.broadcasted_iota(jnp.int32, (R2, R2), 1) < 64
    for h in range(2):
        yh = y_hi[h * 256 : (h + 1) * 256, :]
        yl = y_lo[h * 256 : (h + 1) * 256, :]
        full = lax.dot_general(f2_ref[...], yh, NT, preferred_element_type=F32)
        res = full[0:256] + full[256:512]
        res = res + lax.dot_general(f2_ref[0:256, :], yl, NT, preferred_element_type=F32)
        for j in range(2):
            re = res[0:R2, j * R2 : (j + 1) * R2]
            im = res[R2 : 2 * R2, j * R2 : (j + 1) * R2]
            first = jnp.where(left, re, pltpu.roll(im, 64, 1))
            second = jnp.where(left, pltpu.roll(re, 64, 1), im)
            g = 4 * h + 2 * j
            os[pl.ds(g * group + step, R2, stride=GROUPS * group), :] = first
            os[pl.ds((g + 1) * group + step, R2, stride=GROUPS * group), :] = second


def fft_kernel(group, v_ref, taps_ref, tw_ref, mtw_ref, f2_ref, out_ref, vs, mid, y_hi, y_lo, os):
    step = pl.program_id(1)
    transform(group, step, v_ref, taps_ref, tw_ref, mtw_ref, f2_ref, vs, mid, y_hi, y_lo, os)

    @pl.when(step == group - 1)
    def _():
        n_dest, per_dest = out_ref.shape[0], out_ref.shape[1]

        def emit(dest, carry):
            size = per_dest * group
            part = os[pl.ds(pl.multiple_of(dest * size, size), size), :]
            out_ref[dest] = part.reshape(per_dest, group, R2).astype(BF16)
            return carry

        lax.fori_loop(0, n_dest, emit, 0)


def by_sample(voltages):
    count = voltages.shape[0]
    split = voltages.reshape(count, FRAMES, 2, R1, R2)
    return jnp.transpose(split, (0, 1, 3, 2, 4)).reshape(count, FRAMES, 2 * R1, R2)


def channelize(voltages, filter_taps, devices):
    count = voltages.shape[0]
    group = min(16, count)
    per_dest = OUTCH // devices
    f2, tw, mtw = tables()
    return pl.pallas_call(
        functools.partial(fft_kernel, group),
        grid=(count // group, group),
        out_shape=jax.ShapeDtypeStruct((devices, per_dest, count, R2), BF16),
        in_specs=[
            pl.BlockSpec((None, FRAMES, 2 * R1, R2), lambda i, j: (i * group + j, 0, 0, 0)),
            pl.BlockSpec((TAPS, NFFT), lambda i, j: (0, 0)),
            pl.BlockSpec((R1, 2, R2), lambda i, j: (0, 0, 0)),
            pl.BlockSpec((8, 8, R2), lambda i, j: (0, 0, 0)),
            pl.BlockSpec((512, 256), lambda i, j: (0, 0)),
        ],
        out_specs=pl.BlockSpec((devices, per_dest, group, R2), lambda i, j: (0, 0, i, 0)),
        scratch_shapes=[
            pltpu.VMEM((2 * R1, ROWS, R2), F32),
            pltpu.VMEM((4, 16, SPEC, R2), F32),
            pltpu.VMEM((512, 256), BF16),
            pltpu.VMEM((512, 256), BF16),
            pltpu.VMEM((OUTCH * group, R2), F32),
        ],
        compiler_params=pltpu.CompilerParams(vmem_limit_bytes=48 << 20),
        name="channelize",
    )(
        by_sample(voltages),
        filter_taps,
        jnp.asarray(tw),
        jnp.asarray(mtw),
        jnp.asarray(f2),
    )


def steer(first_channel, stations, gains, delays, wr, wi):
    highest = lax.Precision.HIGHEST
    table = jnp.concatenate([gains / math.sqrt(LIST), delays * (2.0 * math.pi / NFFT)], axis=0)
    beam = lax.broadcasted_iota(jnp.int32, (2 * BEAMS, 1), 0) % BEAMS
    spread = jnp.zeros((2 * BEAMS, STATIONS), F32)
    for b in range(BEAMS):
        named = lax.broadcasted_iota(jnp.int32, (STATIONS, LIST), 0) == stations[b : b + 1, :]
        row = jnp.where(beam == b, table, 0.0)
        spread += lax.dot_general(
            row, named.astype(F32), NT, precision=highest, preferred_element_type=F32
        )
    gain, rate = spread[0:BEAMS], spread[BEAMS:]
    fine = [(jnp.cos(rate * float(f)), jnp.sin(rate * float(f))) for f in range(FAVG)]

    def one(o, carry):
        base = rate * (first_channel + FAVG * o).astype(F32)
        base_cos, base_sin = gain * jnp.cos(base), gain * jnp.sin(base)
        for f, (fine_cos, fine_sin) in enumerate(fine):
            real = base_cos * fine_cos - base_sin * fine_sin
            imag = -(base_sin * fine_cos + base_cos * fine_sin)
            wr[o, f * BEAMS : (f + 1) * BEAMS, :] = real.astype(BF16)
            wi[o, f * BEAMS : (f + 1) * BEAMS, :] = imag.astype(BF16)
        return carry

    lax.fori_loop(0, wr.shape[0], one, 0)


def station_kernel(
    stn, chan, v_ref, taps_ref, tw_ref, mtw_ref, f2_ref, pairs, stations, gain, delay, vis, last, wr, wi, sums,
    vs, mid, y_hi, y_lo, os, stage, x, gains, delays, both, wide,
    send_sem, early_sem, late_sem, own_sem, beam_send, beam_recv, beam_own,
):
    devices = stn * chan
    row, column = lax.axis_index("stn"), lax.axis_index("chan")
    me = row * chan + column
    now = pl.program_id(0)
    per_dest, parts = stage.shape[1], stage.shape[2]
    count = parts * SEND_GROUP
    late = LATE // SEND_GROUP
    early = parts - late
    some = CHUNK
    chunks = per_dest // some
    part, step = now // SEND_GROUP, now % SEND_GROUP
    barrier = pltpu.get_barrier_semaphore()
    small = ((gain, gains), (delay, delays))

    def peer(k):
        dest = lax.rem(me + k, devices)
        return dest, (dest // chan, lax.rem(dest, chan))

    def beam_copy(which, k):
        return pltpu.make_async_remote_copy(
            src_ref=small[which][0],
            dst_ref=small[which][1].at[row],
            send_sem=beam_send.at[which, k],
            recv_sem=beam_recv.at[which, k],
            device_id=(lax.rem(row + k, stn), column),
            device_id_type=pl.DeviceIdType.MESH,
        )

    def beam_keep(which):
        return pltpu.make_async_copy(small[which][0], small[which][1].at[row], beam_own.at[which])

    def copy(k, outs, first, size, sem):
        dest, where = peer(k)
        return pltpu.make_async_remote_copy(
            src_ref=stage.at[dest, outs, pl.ds(first, size)],
            dst_ref=x.at[outs, pl.ds(me * parts + first, size)],
            send_sem=send_sem,
            recv_sem=sem,
            device_id=where,
            device_id_type=pl.DeviceIdType.MESH,
        )

    def own():
        return pltpu.make_async_copy(stage.at[me], x.at[:, pl.ds(me * parts, parts)], own_sem)

    def arrived(outs, size, sem):
        ref = x.at[outs, pl.ds(0, (devices - 1) * size)]
        pltpu.make_async_copy(ref, ref, sem).wait()

    def rows_of(out, k):
        return x[out, pl.ds(k * (BLK // SEND_GROUP), BLK // SEND_GROUP)].reshape(BLK, R2)

    def fill(dest):
        size = per_dest * SEND_GROUP
        rows = os[pl.ds(pl.multiple_of(dest * size, size), size), :]
        stage[dest, :, pl.ds(part, 1)] = rows.reshape(per_dest, 1, SEND_GROUP, R2).astype(BF16)

    @pl.when(now == 0)
    def _():
        def greet(k, carry):
            pl.semaphore_signal(
                barrier, inc=1, device_id=peer(k)[1], device_id_type=pl.DeviceIdType.MESH
            )
            return carry

        lax.fori_loop(1, devices, greet, 0)

    @pl.when(now < count)
    def _():
        transform(SEND_GROUP, step, v_ref, taps_ref, tw_ref, mtw_ref, f2_ref, vs, mid, y_hi, y_lo, os)

    @pl.when(now == SEND_GROUP - 1)
    def _():
        pl.semaphore_wait(barrier, devices - 1)
        for which in range(2):
            for k in range(1, stn):
                beam_copy(which, k).start()
            beam_keep(which).start()

    @pl.when((now < count) & (step == SEND_GROUP - 1) & (part < early))
    def _():
        def emit(k, carry):
            fill(peer(k)[0])
            copy(k, slice(None), part, 1, early_sem).start()
            return carry

        lax.fori_loop(1, devices, emit, 0)
        fill(me)

    @pl.when((now < count) & (step == SEND_GROUP - 1) & (part >= early))
    def _():
        def emit(dest, carry):
            fill(dest)
            return carry

        lax.fori_loop(0, devices, emit, 0)

    @pl.when(now == count - 1)
    def _():
        def emit(n, carry):
            chunk, k = n // (devices - 1), 1 + lax.rem(n, devices - 1)
            copy(k, pl.ds(chunk * some, some), early, late, late_sem.at[chunk]).start()
            return carry

        lax.fori_loop(0, chunks * (devices - 1), emit, 0)
        own().start()
        for which in range(2):
            for k in range(1, stn):
                beam_copy(which, k).wait()
            beam_keep(which).wait()
        every = [jnp.concatenate([ref[r] for r in range(stn)], axis=0) for ref in (gains, delays)]
        steer(me * (per_dest * FAVG), stations[...], every[0], every[1], wr, wi)
        own().wait()
        arrived(slice(None), early, early_sem)

    @pl.when(now >= count)
    def _():
        chunk = now - count
        arrived(pl.ds(chunk * some, some), late, late_sem.at[chunk])

        @pl.when(chunk < chunks - 1)
        def _():
            correlate_chunk(chunk, chunk, pairs, rows_of, wr, wi, vis, both, wide, sums)

    @pl.when(now == count + chunks - 1)
    def _():
        def keep(n, carry):
            o, k = n // NBLK, lax.rem(n, NBLK)
            last[o, pl.ds(pl.multiple_of(k * BLK, BLK), BLK), :] = rows_of((chunks - 1) * some + o, k)
            return carry

        lax.fori_loop(0, some * NBLK, keep, 0)
        sent = stage.at[pl.ds(0, devices - 1)]
        pltpu.make_async_copy(sent, sent, send_sem).wait()


def correlate_chunk(chunk, slot, pairs, rows_of, wr_ref, wi_ref, vis_ref, both, wide, sums):
    some = CHUNK
    lane = lax.broadcasted_iota(jnp.int32, (1, R2), 1)
    sign = jnp.where(lane < 64, -1.0, 1.0).astype(F32)
    of = (lane // SPEC) % FAVG

    def one(o, carry):
        out = chunk * some + o
        for k in range(NBLK):
            x = rows_of(out, k)
            xf = x.astype(F32)
            wide[o, k * BLK : (k + 1) * BLK, :] = xf
            both[o, k, 0:BLK, :] = x
            both[o, k, BLK : 2 * BLK, :] = (pltpu.roll(xf, 64, 1) * sign).astype(BF16)
        for r in range(PAIRS):
            rows = both[o, pairs[0, r], 0:BLK, :]
            vis = lax.dot_general(rows, both[o, pairs[1, r]], NT, preferred_element_type=F32)
            vis_ref[slot * some + o, r] = (vis * (1.0 / (FAVG * SPEC))).astype(BF16)
        for p in range(2):
            x = wide.at[o][pl.ds(p, STATIONS, stride=2), :].astype(BF16)
            real = jnp.dot(wr_ref[out], x, preferred_element_type=F32)
            imag = jnp.dot(wi_ref[out], x, preferred_element_type=F32)
            beams = real + sign * pltpu.roll(imag, 64, 1)
            total = beams[0:BEAMS]
            for f in range(1, FAVG):
                total = jnp.where(of == f, beams[f * BEAMS : (f + 1) * BEAMS], total)
            first = pl.multiple_of((out * 2 + p) * BEAMS, BEAMS)
            sums[pl.ds(first, BEAMS), :] = total
        return carry

    lax.fori_loop(0, some, one, 0)


def finish_kernel(
    pairs_ref, part_ref, x_ref, wr_ref, wi_ref, sums_ref, vis_ref, beam_ref,
    pairs, last, both, wide, sums, beams, pairs_sem, sem, beam_sem,
):
    some = CHUNK
    first = vis_ref.shape[0] - some
    held = first * 2 * BEAMS

    def rows_of(out, k):
        return x_ref[out - first, k * BLK : (k + 1) * BLK, :]

    roster = pltpu.make_async_copy(pairs_ref, pairs, pairs_sem)
    roster.start()
    copies = [
        pltpu.make_async_copy(part_ref.at[pl.ds(0, first)], vis_ref.at[pl.ds(0, first)], sem.at[0]),
        pltpu.make_async_copy(last, vis_ref.at[pl.ds(first, some)], sem.at[1]),
        pltpu.make_async_copy(beams, beam_ref, beam_sem),
    ]
    copies[0].start()
    sums[0:held, :] = sums_ref[0:held, :]
    roster.wait()
    correlate_chunk(first // some, 0, pairs, rows_of, wr_ref, wi_ref, last, both, wide, sums)
    copies[1].start()
    turn_beams(sums, beams)
    copies[2].start()
    for copy in copies:
        copy.wait()


def fused(voltages, filter_taps, stations, gain, delay, block_pairs, stn, chan):
    count = voltages.shape[0]
    devices = stn * chan
    per_dest = OUTCH // devices
    parts = count // SEND_GROUP
    some = CHUNK
    chunks = per_dest // some
    lanes = FAVG * per_dest
    f2, tw, mtw = tables()
    held = [
        pltpu.VMEM((per_dest, PAIRS, BLK, 2 * BLK), BF16),
        pltpu.VMEM((some, INPUTS, R2), BF16),
        pltpu.VMEM((per_dest, FAVG * BEAMS, STATIONS), BF16),
        pltpu.VMEM((per_dest, FAVG * BEAMS, STATIONS), BF16),
        pltpu.VMEM((per_dest * 2 * BEAMS, R2), F32),
    ]
    worked = pl.pallas_call(
        functools.partial(station_kernel, stn, chan),
        grid=(count + chunks,),
        out_shape=held,
        in_specs=[
            pl.BlockSpec((None, FRAMES, 2 * R1, R2), lambda i: (jnp.minimum(i, count - 1), 0, 0, 0)),
            pl.BlockSpec((TAPS, NFFT), lambda i: (0, 0)),
            pl.BlockSpec((R1, 2, R2), lambda i: (0, 0, 0)),
            pl.BlockSpec((8, 8, R2), lambda i: (0, 0, 0)),
            pl.BlockSpec((512, 256), lambda i: (0, 0)),
            pl.BlockSpec(memory_space=pltpu.SMEM),
            pl.BlockSpec((BEAMS, LIST), lambda i: (0, 0)),
            pl.BlockSpec(memory_space=pl.ANY),
            pl.BlockSpec(memory_space=pl.ANY),
        ],
        out_specs=[pl.BlockSpec(memory_space=pltpu.VMEM)] * len(held),
        scratch_shapes=[
            pltpu.VMEM((2 * R1, ROWS, R2), F32),
            pltpu.VMEM((4, 16, SPEC, R2), F32),
            pltpu.VMEM((512, 256), BF16),
            pltpu.VMEM((512, 256), BF16),
            pltpu.VMEM((OUTCH * SEND_GROUP, R2), F32),
            pltpu.VMEM((devices, per_dest, parts, SEND_GROUP, R2), BF16),
            pltpu.VMEM((per_dest, devices * parts, SEND_GROUP, R2), BF16),
            pltpu.VMEM((stn,) + gain.shape, F32),
            pltpu.VMEM((stn,) + delay.shape, F32),
            pltpu.VMEM((some, NBLK, 2 * BLK, R2), BF16),
            pltpu.VMEM((some, INPUTS, R2), F32),
            pltpu.SemaphoreType.DMA,
            pltpu.SemaphoreType.DMA,
            pltpu.SemaphoreType.DMA((chunks,)),
            pltpu.SemaphoreType.DMA,
            pltpu.SemaphoreType.DMA((2, stn)),
            pltpu.SemaphoreType.DMA((2, stn)),
            pltpu.SemaphoreType.DMA((2,)),
        ],
        compiler_params=pltpu.CompilerParams(
            vmem_limit_bytes=48 << 20, collective_id=0, has_side_effects=True
        ),
        name="station_beamformer",
    )(
        by_sample(voltages),
        filter_taps,
        jnp.asarray(tw),
        jnp.asarray(mtw),
        jnp.asarray(f2),
        block_pairs.T,
        stations,
        gain,
        delay,
    )
    whole = pl.BlockSpec(memory_space=pltpu.VMEM)
    visibilities, beams = pl.pallas_call(
        finish_kernel,
        out_shape=[
            jax.ShapeDtypeStruct((per_dest, PAIRS, BLK, 2 * BLK), BF16),
            jax.ShapeDtypeStruct((BEAMS, 2, 2 * SPEC, lanes), BF16),
        ],
        in_specs=[pl.BlockSpec(memory_space=pl.ANY)] + [whole] * len(held),
        out_specs=[pl.BlockSpec(memory_space=pl.ANY)] * 2,
        scratch_shapes=[
            pltpu.SMEM((2, PAIRS), jnp.int32),
            pltpu.VMEM((some, PAIRS, BLK, 2 * BLK), BF16),
            pltpu.VMEM((some, NBLK, 2 * BLK, R2), BF16),
            pltpu.VMEM((some, INPUTS, R2), F32),
            pltpu.VMEM((per_dest * 2 * BEAMS, R2), F32),
            pltpu.VMEM((BEAMS, 2, 2 * SPEC, lanes), BF16),
            pltpu.SemaphoreType.DMA,
            pltpu.SemaphoreType.DMA((2,)),
            pltpu.SemaphoreType.DMA,
        ],
        compiler_params=pltpu.CompilerParams(vmem_limit_bytes=16 << 20),
        name="finish",
    )(block_pairs.T, *worked)
    return visibilities, jnp.swapaxes(beams, 2, 3)


def spectra_of_channels(voltages, filter_taps, gain, delay, stn, chan):
    count = voltages.shape[0]
    devices = stn * chan
    per_dest = OUTCH // devices
    spectra = channelize(voltages, filter_taps, devices)
    moved = lax.all_to_all(spectra, ("stn", "chan"), split_axis=0, concat_axis=0, tiled=True)
    turned = jnp.transpose(moved, (1, 0, 2, 3)).reshape(per_dest, devices * count, R2)
    gains = lax.all_gather(gain, "stn", axis=0, tiled=True)
    delays = lax.all_gather(delay, "stn", axis=0, tiled=True)
    return turned, gains, delays


def correlate_kernel(pairs, x_ref, wr_ref, wi_ref, vis_ref, beam_ref, both, wide, sums):
    chunk = pl.program_id(0)
    some = x_ref.shape[0]
    lane = lax.broadcasted_iota(jnp.int32, (1, R2), 1)
    sign = jnp.where(lane < 64, -1.0, 1.0).astype(F32)
    of = (lane // SPEC) % FAVG
    for o in range(some):
        for k in range(NBLK):
            x = x_ref[o, k * BLK : (k + 1) * BLK, :]
            xf = x.astype(F32)
            wide[o, k * BLK : (k + 1) * BLK, :] = xf
            both[o, k, 0:BLK, :] = x
            both[o, k, BLK : 2 * BLK, :] = (pltpu.roll(xf, 64, 1) * sign).astype(BF16)
        for r in range(PAIRS):
            rows = both[o, pairs[0, r], 0:BLK, :]
            vis = lax.dot_general(rows, both[o, pairs[1, r]], NT, preferred_element_type=F32)
            vis_ref[o, r] = (vis * (1.0 / (FAVG * SPEC))).astype(BF16)
        for p in range(2):
            x = wide.at[o][pl.ds(p, STATIONS, stride=2), :].astype(BF16)
            real = jnp.dot(wr_ref[o], x, preferred_element_type=F32)
            imag = jnp.dot(wi_ref[o], x, preferred_element_type=F32)
            beams = real + sign * pltpu.roll(imag, 64, 1)
            total = beams[0:BEAMS]
            for f in range(1, FAVG):
                total = jnp.where(of == f, beams[f * BEAMS : (f + 1) * BEAMS], total)
            first = pl.multiple_of(((chunk * some + o) * 2 + p) * BEAMS, BEAMS)
            sums[pl.ds(first, BEAMS), :] = total

    @pl.when(chunk == pl.num_programs(0) - 1)
    def _():
        turn_beams(sums, beam_ref)


def turn_beams(sums, beam_ref):
    lanes = beam_ref.shape[3]
    count = lanes // FAVG
    column = lax.broadcasted_iota(jnp.int32, (count, lanes), 1)
    spread = jnp.where(column // FAVG == lax.broadcasted_iota(jnp.int32, (count, lanes), 0), 1.0, 0.0)
    spread = spread.astype(BF16)
    fine = lax.broadcasted_iota(jnp.int32, (1, lanes), 1) % FAVG
    for p in range(2):
        for b in range(BEAMS):
            rows = sums[pl.ds(p * BEAMS + b, count, stride=2 * BEAMS), :].astype(BF16)
            moved = lax.dot_general(rows, spread, TN, preferred_element_type=F32)
            for q in range(2):
                total = moved[q * 64 : q * 64 + SPEC]
                for f in range(1, FAVG):
                    total = jnp.where(fine == f, moved[q * 64 + f * SPEC : q * 64 + (f + 1) * SPEC], total)
                beam_ref[b, p, q * SPEC : (q + 1) * SPEC, :] = total.astype(BF16)


def correlate(turned, real, imag, block_pairs):
    per_dest = turned.shape[0]
    lanes = FAVG * per_dest
    some = math.gcd(per_dest, 4)
    weight_spec = pl.BlockSpec((some, FAVG * BEAMS, STATIONS), lambda o, pairs: (o, 0, 0))
    visibilities, beams = pl.pallas_call(
        correlate_kernel,
        grid_spec=pltpu.PrefetchScalarGridSpec(
            num_scalar_prefetch=1,
            grid=(per_dest // some,),
            in_specs=[
                pl.BlockSpec((some, INPUTS, R2), lambda o, pairs: (o, 0, 0)),
                weight_spec,
                weight_spec,
            ],
            out_specs=[
                pl.BlockSpec((some, PAIRS, BLK, 2 * BLK), lambda o, pairs: (o, 0, 0, 0)),
                pl.BlockSpec((BEAMS, 2, 2 * SPEC, lanes), lambda o, pairs: (0, 0, 0, 0)),
            ],
            scratch_shapes=[
                pltpu.VMEM((some, NBLK, 2 * BLK, R2), BF16),
                pltpu.VMEM((some, INPUTS, R2), F32),
                pltpu.VMEM((per_dest * 2 * BEAMS, R2), F32),
            ],
        ),
        out_shape=[
            jax.ShapeDtypeStruct((per_dest, PAIRS, BLK, 2 * BLK), BF16),
            jax.ShapeDtypeStruct((BEAMS, 2, 2 * SPEC, lanes), BF16),
        ],
        name="correlate",
    )(block_pairs.T, turned, real, imag)
    return visibilities, jnp.swapaxes(beams, 2, 3)


def beam_weights(stations, gains, delays, chan_start, per_dest):
    named = stations[:, :, None] == jnp.arange(STATIONS, dtype=jnp.int32)[None, None, :]
    gain = jnp.sum(jnp.where(named, gains[:, :, None] / math.sqrt(LIST), 0.0), axis=1)
    delay = jnp.sum(jnp.where(named, delays[:, :, None], 0.0), axis=1)
    rate = 2.0 * math.pi / NFFT * delay
    coarse = (chan_start + FAVG * jnp.arange(per_dest, dtype=jnp.int32)).astype(F32)
    base = rate[None] * coarse[:, None, None]
    base_cos, base_sin = gain * jnp.cos(base), gain * jnp.sin(base)
    fine = rate[None] * jnp.arange(FAVG, dtype=jnp.int32).astype(F32)[:, None, None]
    fine_cos, fine_sin = jnp.cos(fine)[None], jnp.sin(fine)[None]
    base_cos, base_sin = base_cos[:, None], base_sin[:, None]
    real = base_cos * fine_cos - base_sin * fine_sin
    imag = -(base_sin * fine_cos + base_cos * fine_sin)
    shape = (per_dest, FAVG * BEAMS, STATIONS)
    return real.astype(BF16).reshape(shape), imag.astype(BF16).reshape(shape)


def shards(voltages, filter_taps, beam_stations, beam_gain, beam_delay, block_pairs):
    stn = lax.axis_size("stn")
    chan = lax.axis_size("chan")
    devices = stn * chan
    per_dest = OUTCH // devices
    chan_start = (lax.axis_index("stn") * chan + lax.axis_index("chan")) * (NFFT // devices)
    if voltages.shape[0] % SEND_GROUP == 0 and voltages.shape[0] > LATE and per_dest % CHUNK == 0:
        return fused(
            voltages, filter_taps, beam_stations, beam_gain, beam_delay, block_pairs, stn, chan
        )
    turned, gains, delays = spectra_of_channels(
        voltages, filter_taps, beam_gain, beam_delay, stn, chan
    )
    real, imag = beam_weights(beam_stations, gains, delays, chan_start, per_dest)
    return correlate(turned, real, imag, block_pairs)


def solution(mesh):
    placed = (P(("stn", "chan"), None, None, None), P(), P(), P("stn", None), P("stn", None), P())
    return jax.shard_map(
        shards,
        mesh=mesh,
        in_specs=placed,
        out_specs=(P(("stn", "chan"), None, None, None), P(None, None, ("stn", "chan"), None)),
        check_vma=False,
    )
```

```python
import functools
import math

import jax
import jax.numpy as jnp
import numpy as np
from jax import lax
from jax.experimental import pallas as pl
from jax.experimental.pallas import tpu as pltpu
from jax.sharding import PartitionSpec as P

STATIONS = 512
INPUTS = 1024
NFFT = 4096
BEAMS = 16
TAPS = 12
FAVG = 4
BLK = 64
LIST = 128
SPEC = 16
FRAMES = 27
NBLK = 16
PAIRS = 16
R1 = 32
R2 = 128
GROUPS = R1 // FAVG
OUTCH = NFFT // FAVG
SEND_GROUP = 2
LATE = 20
CHUNK = 2
ROWS = 40
PITCH = 24
SUMS = 40
F32 = jnp.float32
BF16 = jnp.bfloat16
NT = (((1,), (1,)), ((), ()))
TN = (((0,), (0,)), ((), ()))


def tables():
    b = np.arange(R2)
    ang = 2.0 * np.pi * (b[:, None] * b[None, :] % R2) / R2
    f2 = np.block([[np.cos(ang), np.sin(ang)], [-np.sin(ang), np.cos(ang)]])
    hi = f2.astype(jnp.bfloat16)
    lo = (f2 - hi.astype(np.float64)).astype(jnp.bfloat16)
    f2 = np.concatenate([hi, lo], axis=0)
    ang = 2.0 * np.pi * (np.arange(R1)[:, None] * b[None, :]) / NFFT
    tw = np.stack([np.cos(ang), -np.sin(ang)], axis=1) / math.sqrt(NFFT)
    ang = 2.0 * np.pi * (np.arange(8)[:, None] * np.arange(4)[None, :]) / R1
    mid = np.stack([np.cos(ang), -np.sin(ang)], axis=-1).reshape(8, 8, 1)
    mid = np.broadcast_to(mid, (8, 8, R2))
    return f2, tw.astype(np.float32), mid.astype(np.float32)


def add(x, y):
    return (x[0] + y[0], x[1] + y[1])


def sub(x, y):
    return (x[0] - y[0], x[1] - y[1])


def turn(x):
    return (x[1], -x[0])


def dft4(x):
    p, m = add(x[0], x[2]), sub(x[0], x[2])
    q, n = add(x[1], x[3]), turn(sub(x[1], x[3]))
    return [add(p, q), add(m, n), sub(p, q), sub(m, n)]


def dft8(x):
    even = dft4(x[0::2])
    odd = dft4(x[1::2])
    h = math.sqrt(0.5)
    o1, o3 = odd[1], odd[3]
    odd = [
        odd[0],
        ((o1[0] + o1[1]) * h, (o1[1] - o1[0]) * h),
        turn(odd[2]),
        ((o3[1] - o3[0]) * h, -(o3[0] + o3[1]) * h),
    ]
    return [add(e, o) for e, o in zip(even, odd)] + [sub(e, o) for e, o in zip(even, odd)]


def transform(group, pitch, step, v_ref, taps_ref, tw_ref, mtw_ref, f2_ref, vs, mid, y_hi, y_lo, os):
    rows = vs.reshape(2 * R1 * ROWS, R2)
    for frame in range(FRAMES):
        rows[pl.ds(frame, 2 * R1, stride=ROWS), :] = v_ref[frame].astype(F32)

    def low(a_lo, carry):
        x = []
        for a_hi in range(4):
            a = a_lo + 8 * a_hi
            parts = [None, None]
            for t in range(TAPS):
                tap = taps_ref[t : t + 1, pl.ds(pl.multiple_of(a * R2, R2), R2)]
                for q in range(2):
                    term = tap * vs[2 * a + q, t : t + SPEC, :]
                    parts[q] = term if t == 0 else parts[q] + term
            x.append(tuple(parts))
        z = dft4(x)
        for k in range(4):
            zr, zi = z[k]
            if k:
                wr = mtw_ref[a_lo, 2 * k : 2 * k + 1, :]
                wi = mtw_ref[a_lo, 2 * k + 1 : 2 * k + 2, :]
                zr, zi = zr * wr - zi * wi, zr * wi + zi * wr
            mid[k, 2 * a_lo] = zr
            mid[k, 2 * a_lo + 1] = zi
        return carry

    lax.fori_loop(0, 8, low, 0)
    for k in range(4):
        z = dft8([(mid[k, 2 * a], mid[k, 2 * a + 1]) for a in range(8)])
        for k2 in range(8):
            c1 = k + 4 * k2
            zr, zi = z[k2]
            wr, wi = tw_ref[c1, 0:1, :], tw_ref[c1, 1:2, :]
            for q, val in enumerate((zr * wr - zi * wi, zr * wi + zi * wr)):
                hi = val.astype(BF16)
                y_hi[c1 * SPEC : (c1 + 1) * SPEC, q * R2 : (q + 1) * R2] = hi
                y_lo[c1 * SPEC : (c1 + 1) * SPEC, q * R2 : (q + 1) * R2] = (
                    val - hi.astype(F32)
                ).astype(BF16)
    left = lax.broadcasted_iota(jnp.int32, (R2, R2), 1) < 64
    for h in range(2):
        yh = y_hi[h * 256 : (h + 1) * 256, :]
        yl = y_lo[h * 256 : (h + 1) * 256, :]
        full = lax.dot_general(f2_ref[...], yh, NT, preferred_element_type=F32)
        res = full[0:256] + full[256:512]
        res = res + lax.dot_general(f2_ref[0:256, :], yl, NT, preferred_element_type=F32)
        for j in range(2):
            re = res[0:R2, j * R2 : (j + 1) * R2]
            im = res[R2 : 2 * R2, j * R2 : (j + 1) * R2]
            first = jnp.where(left, re, pltpu.roll(im, 64, 1))
            second = jnp.where(left, pltpu.roll(re, 64, 1), im)
            g = 4 * h + 2 * j
            os[pl.ds(g * group + step, R2, stride=pitch), :] = first
            os[pl.ds((g + 1) * group + step, R2, stride=pitch), :] = second


def fft_kernel(group, v_ref, taps_ref, tw_ref, mtw_ref, f2_ref, out_ref, vs, mid, y_hi, y_lo, os):
    step = pl.program_id(1)
    transform(group, GROUPS * group, step, v_ref, taps_ref, tw_ref, mtw_ref, f2_ref, vs, mid, y_hi, y_lo, os)

    @pl.when(step == group - 1)
    def _():
        n_dest, per_dest = out_ref.shape[0], out_ref.shape[1]

        def emit(dest, carry):
            size = per_dest * group
            part = os[pl.ds(pl.multiple_of(dest * size, size), size), :]
            out_ref[dest] = part.reshape(per_dest, group, R2).astype(BF16)
            return carry

        lax.fori_loop(0, n_dest, emit, 0)


def by_sample(voltages):
    count = voltages.shape[0]
    split = voltages.reshape(count, FRAMES, 2, R1, R2)
    return jnp.transpose(split, (0, 1, 3, 2, 4)).reshape(count, FRAMES, 2 * R1, R2)


def channelize(voltages, filter_taps, devices):
    count = voltages.shape[0]
    group = min(16, count)
    per_dest = OUTCH // devices
    f2, tw, mtw = tables()
    return pl.pallas_call(
        functools.partial(fft_kernel, group),
        grid=(count // group, group),
        out_shape=jax.ShapeDtypeStruct((devices, per_dest, count, R2), BF16),
        in_specs=[
            pl.BlockSpec((None, FRAMES, 2 * R1, R2), lambda i, j: (i * group + j, 0, 0, 0)),
            pl.BlockSpec((TAPS, NFFT), lambda i, j: (0, 0)),
            pl.BlockSpec((R1, 2, R2), lambda i, j: (0, 0, 0)),
            pl.BlockSpec((8, 8, R2), lambda i, j: (0, 0, 0)),
            pl.BlockSpec((512, 256), lambda i, j: (0, 0)),
        ],
        out_specs=pl.BlockSpec((devices, per_dest, group, R2), lambda i, j: (0, 0, i, 0)),
        scratch_shapes=[
            pltpu.VMEM((2 * R1, ROWS, R2), F32),
            pltpu.VMEM((4, 16, SPEC, R2), F32),
            pltpu.VMEM((512, 256), BF16),
            pltpu.VMEM((512, 256), BF16),
            pltpu.VMEM((OUTCH * group, R2), F32),
        ],
        compiler_params=pltpu.CompilerParams(vmem_limit_bytes=48 << 20),
        name="channelize",
    )(
        by_sample(voltages),
        filter_taps,
        jnp.asarray(tw),
        jnp.asarray(mtw),
        jnp.asarray(f2),
    )


def steer(first_channel, stations, gains, delays, wr, wi):
    highest = lax.Precision.HIGHEST
    table = jnp.concatenate([gains / math.sqrt(LIST), delays * (2.0 * math.pi / NFFT)], axis=0)
    beam = lax.broadcasted_iota(jnp.int32, (2 * BEAMS, 1), 0) % BEAMS
    spread = jnp.zeros((2 * BEAMS, STATIONS), F32)
    for b in range(BEAMS):
        named = lax.broadcasted_iota(jnp.int32, (STATIONS, LIST), 0) == stations[b : b + 1, :]
        row = jnp.where(beam == b, table, 0.0)
        spread += lax.dot_general(
            row, named.astype(F32), NT, precision=highest, preferred_element_type=F32
        )
    gain, rate = spread[0:BEAMS], spread[BEAMS:]
    fine = [(jnp.cos(rate * float(f)), jnp.sin(rate * float(f))) for f in range(FAVG)]

    def one(o, carry):
        base = rate * (first_channel + FAVG * o).astype(F32)
        base_cos, base_sin = gain * jnp.cos(base), gain * jnp.sin(base)
        for f, (fine_cos, fine_sin) in enumerate(fine):
            real = base_cos * fine_cos - base_sin * fine_sin
            imag = -(base_sin * fine_cos + base_cos * fine_sin)
            wr[o, f * BEAMS : (f + 1) * BEAMS, :] = real.astype(BF16)
            wi[o, f * BEAMS : (f + 1) * BEAMS, :] = imag.astype(BF16)
        return carry

    lax.fori_loop(0, wr.shape[0], one, 0)


def station_kernel(
    stn, chan, v_ref, taps_ref, tw_ref, mtw_ref, f2_ref, pairs, stations, gain, delay, vis, last, wr, wi, sums,
    vs, mid, y_hi, y_lo, os, stage, x, gains, delays, both, wide,
    send_sem, early_sem, late_sem, own_sem, beam_send, beam_recv, beam_own,
):
    devices = stn * chan
    row, column = lax.axis_index("stn"), lax.axis_index("chan")
    me = row * chan + column
    now = pl.program_id(0)
    per_dest, parts = stage.shape[1], stage.shape[2]
    count = parts * SEND_GROUP
    late = LATE // SEND_GROUP
    early = parts - late
    some = CHUNK
    chunks = per_dest // some
    part, step = now // SEND_GROUP, now % SEND_GROUP
    barrier = pltpu.get_barrier_semaphore()
    small = ((gain, gains), (delay, delays))

    def peer(k):
        dest = lax.rem(me + k, devices)
        return dest, (dest // chan, lax.rem(dest, chan))

    def beam_copy(which, k):
        return pltpu.make_async_remote_copy(
            src_ref=small[which][0],
            dst_ref=small[which][1].at[row],
            send_sem=beam_send.at[which, k],
            recv_sem=beam_recv.at[which, k],
            device_id=(lax.rem(row + k, stn), column),
            device_id_type=pl.DeviceIdType.MESH,
        )

    def beam_keep(which):
        return pltpu.make_async_copy(small[which][0], small[which][1].at[row], beam_own.at[which])

    def copy(k, outs, first, size, sem):
        dest, where = peer(k)
        return pltpu.make_async_remote_copy(
            src_ref=stage.at[dest, outs, pl.ds(first, size)],
            dst_ref=x.at[outs, pl.ds(me * parts + first, size)],
            send_sem=send_sem,
            recv_sem=sem,
            device_id=where,
            device_id_type=pl.DeviceIdType.MESH,
        )

    def own():
        return pltpu.make_async_copy(stage.at[me], x.at[:, pl.ds(me * parts, parts)], own_sem)

    def arrived(outs, size, sem):
        ref = x.at[outs, pl.ds(0, (devices - 1) * size)]
        pltpu.make_async_copy(ref, ref, sem).wait()

    def rows_of(out, k):
        return x[out, pl.ds(k * (BLK // SEND_GROUP), BLK // SEND_GROUP)].reshape(BLK, R2)

    def fill(dest):
        size = per_dest // GROUPS
        rows = [
            os[pl.ds(pl.multiple_of((dest * size + n) * PITCH, 8), GROUPS * SEND_GROUP), :]
            for n in range(size)
        ]
        for n in range(size):
            some_rows = rows[n].reshape(GROUPS, 1, SEND_GROUP, R2).astype(BF16)
            stage[dest, n * GROUPS : (n + 1) * GROUPS, pl.ds(part, 1)] = some_rows

    @pl.when(now == 0)
    def _():
        def greet(k, carry):
            pl.semaphore_signal(
                barrier, inc=1, device_id=peer(k)[1], device_id_type=pl.DeviceIdType.MESH
            )
            return carry

        lax.fori_loop(1, devices, greet, 0)

    @pl.when(now < count)
    def _():
        transform(SEND_GROUP, PITCH, step, v_ref, taps_ref, tw_ref, mtw_ref, f2_ref, vs, mid, y_hi, y_lo, os)

    @pl.when(now == SEND_GROUP - 1)
    def _():
        pl.semaphore_wait(barrier, devices - 1)
        for which in range(2):
            for k in range(1, stn):
                beam_copy(which, k).start()
            beam_keep(which).start()

    @pl.when((now < count) & (step == SEND_GROUP - 1) & (part < early))
    def _():
        def emit(k, carry):
            fill(peer(k)[0])
            copy(k, slice(None), part, 1, early_sem).start()
            return carry

        lax.fori_loop(1, devices, emit, 0)
        fill(me)

    @pl.when((now < count) & (step == SEND_GROUP - 1) & (part >= early))
    def _():
        def emit(dest, carry):
            fill(dest)
            return carry

        lax.fori_loop(0, devices, emit, 0)

    @pl.when(now == count - 1)
    def _():
        def emit(n, carry):
            chunk, k = n // (devices - 1), 1 + lax.rem(n, devices - 1)
            copy(k, pl.ds(chunk * some, some), early, late, late_sem.at[chunk]).start()
            return carry

        lax.fori_loop(0, chunks * (devices - 1), emit, 0)
        own().start()
        for which in range(2):
            for k in range(1, stn):
                beam_copy(which, k).wait()
            beam_keep(which).wait()
        every = [jnp.concatenate([ref[r] for r in range(stn)], axis=0) for ref in (gains, delays)]
        steer(me * (per_dest * FAVG), stations[...], every[0], every[1], wr, wi)
        own().wait()
        arrived(slice(None), early, early_sem)

    @pl.when(now >= count)
    def _():
        chunk = now - count
        arrived(pl.ds(chunk * some, some), late, late_sem.at[chunk])

        @pl.when(chunk < chunks - 1)
        def _():
            correlate_chunk(chunk, chunk, pairs, rows_of, wr, wi, vis, both, wide, sums)

    @pl.when(now == count + chunks - 1)
    def _():
        def keep(n, carry):
            o, k = n // NBLK, lax.rem(n, NBLK)
            last[o, pl.ds(pl.multiple_of(k * BLK, BLK), BLK), :] = rows_of((chunks - 1) * some + o, k)
            return carry

        lax.fori_loop(0, some * NBLK, keep, 0)
        sent = stage.at[pl.ds(0, devices - 1)]
        pltpu.make_async_copy(sent, sent, send_sem).wait()


def correlate_chunk(chunk, slot, pairs, rows_of, wr_ref, wi_ref, vis_ref, both, wide, sums):
    some = CHUNK
    lane = lax.broadcasted_iota(jnp.int32, (1, R2), 1)
    sign = jnp.where(lane < 64, -1.0, 1.0).astype(F32)
    of = (lane // SPEC) % FAVG

    def one(o, carry):
        out = chunk * some + o
        for k in range(NBLK):
            x = rows_of(out, k)
            xf = x.astype(F32)
            wide[o, k * BLK : (k + 1) * BLK, :] = xf
            both[o, k, 0:BLK, :] = x
            both[o, k, BLK : 2 * BLK, :] = (pltpu.roll(xf, 64, 1) * sign).astype(BF16)
        for r in range(PAIRS):
            rows = both[o, pairs[0, r], 0:BLK, :]
            vis = lax.dot_general(rows, both[o, pairs[1, r]], NT, preferred_element_type=F32)
            vis_ref[slot * some + o, r] = (vis * (1.0 / (FAVG * SPEC))).astype(BF16)
        for p in range(2):
            x = wide.at[o][pl.ds(p, STATIONS, stride=2), :].astype(BF16)
            real = jnp.dot(wr_ref[out], x, preferred_element_type=F32)
            imag = jnp.dot(wi_ref[out], x, preferred_element_type=F32)
            beams = real + sign * pltpu.roll(imag, 64, 1)
            total = beams[0:BEAMS]
            for f in range(1, FAVG):
                total = jnp.where(of == f, beams[f * BEAMS : (f + 1) * BEAMS], total)
            first = pl.multiple_of(out * SUMS + p * BEAMS, 8)
            sums[pl.ds(first, BEAMS), :] = total
        return carry

    lax.fori_loop(0, some, one, 0)


def finish_kernel(
    pairs_ref, part_ref, x_ref, wr_ref, wi_ref, sums_ref, vis_ref, beam_ref,
    pairs, last, both, wide, sums, beams, pairs_sem, sem, beam_sem,
):
    some = CHUNK
    first = vis_ref.shape[0] - some
    held = first * SUMS

    def rows_of(out, k):
        return x_ref[out - first, k * BLK : (k + 1) * BLK, :]

    roster = pltpu.make_async_copy(pairs_ref, pairs, pairs_sem)
    roster.start()
    copies = [
        pltpu.make_async_copy(part_ref.at[pl.ds(0, first)], vis_ref.at[pl.ds(0, first)], sem.at[0]),
        pltpu.make_async_copy(last, vis_ref.at[pl.ds(first, some)], sem.at[1]),
        pltpu.make_async_copy(beams, beam_ref, beam_sem),
    ]
    copies[0].start()
    sums[0:held, :] = sums_ref[0:held, :]
    roster.wait()
    correlate_chunk(first // some, 0, pairs, rows_of, wr_ref, wi_ref, last, both, wide, sums)
    copies[1].start()
    turn_beams(sums, SUMS, beams)
    copies[2].start()
    for copy in copies:
        copy.wait()


def fused(voltages, filter_taps, stations, gain, delay, block_pairs, stn, chan):
    count = voltages.shape[0]
    devices = stn * chan
    per_dest = OUTCH // devices
    parts = count // SEND_GROUP
    some = CHUNK
    chunks = per_dest // some
    lanes = FAVG * per_dest
    f2, tw, mtw = tables()
    held = [
        pltpu.VMEM((per_dest, PAIRS, BLK, 2 * BLK), BF16),
        pltpu.VMEM((some, INPUTS, R2), BF16),
        pltpu.VMEM((per_dest, FAVG * BEAMS, STATIONS), BF16),
        pltpu.VMEM((per_dest, FAVG * BEAMS, STATIONS), BF16),
        pltpu.VMEM((per_dest * SUMS, R2), F32),
    ]
    worked = pl.pallas_call(
        functools.partial(station_kernel, stn, chan),
        grid=(count + chunks,),
        out_shape=held,
        in_specs=[
            pl.BlockSpec((None, FRAMES, 2 * R1, R2), lambda i: (jnp.minimum(i, count - 1), 0, 0, 0)),
            pl.BlockSpec((TAPS, NFFT), lambda i: (0, 0)),
            pl.BlockSpec((R1, 2, R2), lambda i: (0, 0, 0)),
            pl.BlockSpec((8, 8, R2), lambda i: (0, 0, 0)),
            pl.BlockSpec((512, 256), lambda i: (0, 0)),
            pl.BlockSpec(memory_space=pltpu.SMEM),
            pl.BlockSpec((BEAMS, LIST), lambda i: (0, 0)),
            pl.BlockSpec(memory_space=pl.ANY),
            pl.BlockSpec(memory_space=pl.ANY),
        ],
        out_specs=[pl.BlockSpec(memory_space=pltpu.VMEM)] * len(held),
        scratch_shapes=[
            pltpu.VMEM((2 * R1, ROWS, R2), F32),
            pltpu.VMEM((4, 16, SPEC, R2), F32),
            pltpu.VMEM((512, 256), BF16),
            pltpu.VMEM((512, 256), BF16),
            pltpu.VMEM((R2 * PITCH, R2), F32),
            pltpu.VMEM((devices, per_dest, parts, SEND_GROUP, R2), BF16),
            pltpu.VMEM((per_dest, devices * parts, SEND_GROUP, R2), BF16),
            pltpu.VMEM((stn,) + gain.shape, F32),
            pltpu.VMEM((stn,) + delay.shape, F32),
            pltpu.VMEM((some, NBLK, 2 * BLK, R2), BF16),
            pltpu.VMEM((some, INPUTS, R2), F32),
            pltpu.SemaphoreType.DMA,
            pltpu.SemaphoreType.DMA,
            pltpu.SemaphoreType.DMA((chunks,)),
            pltpu.SemaphoreType.DMA,
            pltpu.SemaphoreType.DMA((2, stn)),
            pltpu.SemaphoreType.DMA((2, stn)),
            pltpu.SemaphoreType.DMA((2,)),
        ],
        compiler_params=pltpu.CompilerParams(
            vmem_limit_bytes=48 << 20, collective_id=0, has_side_effects=True
        ),
        name="station_beamformer",
    )(
        by_sample(voltages),
        filter_taps,
        jnp.asarray(tw),
        jnp.asarray(mtw),
        jnp.asarray(f2),
        block_pairs.T,
        stations,
        gain,
        delay,
    )
    whole = pl.BlockSpec(memory_space=pltpu.VMEM)
    visibilities, beams = pl.pallas_call(
        finish_kernel,
        out_shape=[
            jax.ShapeDtypeStruct((per_dest, PAIRS, BLK, 2 * BLK), BF16),
            jax.ShapeDtypeStruct((BEAMS, 2, 2 * SPEC, lanes), BF16),
        ],
        in_specs=[pl.BlockSpec(memory_space=pl.ANY)] + [whole] * len(held),
        out_specs=[pl.BlockSpec(memory_space=pl.ANY)] * 2,
        scratch_shapes=[
            pltpu.SMEM((2, PAIRS), jnp.int32),
            pltpu.VMEM((some, PAIRS, BLK, 2 * BLK), BF16),
            pltpu.VMEM((some, NBLK, 2 * BLK, R2), BF16),
            pltpu.VMEM((some, INPUTS, R2), F32),
            pltpu.VMEM((per_dest * SUMS, R2), F32),
            pltpu.VMEM((BEAMS, 2, 2 * SPEC, lanes), BF16),
            pltpu.SemaphoreType.DMA,
            pltpu.SemaphoreType.DMA((2,)),
            pltpu.SemaphoreType.DMA,
        ],
        compiler_params=pltpu.CompilerParams(vmem_limit_bytes=16 << 20),
        name="finish",
    )(block_pairs.T, *worked)
    return visibilities, jnp.swapaxes(beams, 2, 3)


def spectra_of_channels(voltages, filter_taps, gain, delay, stn, chan):
    count = voltages.shape[0]
    devices = stn * chan
    per_dest = OUTCH // devices
    spectra = channelize(voltages, filter_taps, devices)
    moved = lax.all_to_all(spectra, ("stn", "chan"), split_axis=0, concat_axis=0, tiled=True)
    turned = jnp.transpose(moved, (1, 0, 2, 3)).reshape(per_dest, devices * count, R2)
    gains = lax.all_gather(gain, "stn", axis=0, tiled=True)
    delays = lax.all_gather(delay, "stn", axis=0, tiled=True)
    return turned, gains, delays


def correlate_kernel(pairs, x_ref, wr_ref, wi_ref, vis_ref, beam_ref, both, wide, sums):
    chunk = pl.program_id(0)
    some = x_ref.shape[0]
    lane = lax.broadcasted_iota(jnp.int32, (1, R2), 1)
    sign = jnp.where(lane < 64, -1.0, 1.0).astype(F32)
    of = (lane // SPEC) % FAVG
    for o in range(some):
        for k in range(NBLK):
            x = x_ref[o, k * BLK : (k + 1) * BLK, :]
            xf = x.astype(F32)
            wide[o, k * BLK : (k + 1) * BLK, :] = xf
            both[o, k, 0:BLK, :] = x
            both[o, k, BLK : 2 * BLK, :] = (pltpu.roll(xf, 64, 1) * sign).astype(BF16)
        for r in range(PAIRS):
            rows = both[o, pairs[0, r], 0:BLK, :]
            vis = lax.dot_general(rows, both[o, pairs[1, r]], NT, preferred_element_type=F32)
            vis_ref[o, r] = (vis * (1.0 / (FAVG * SPEC))).astype(BF16)
        for p in range(2):
            x = wide.at[o][pl.ds(p, STATIONS, stride=2), :].astype(BF16)
            real = jnp.dot(wr_ref[o], x, preferred_element_type=F32)
            imag = jnp.dot(wi_ref[o], x, preferred_element_type=F32)
            beams = real + sign * pltpu.roll(imag, 64, 1)
            total = beams[0:BEAMS]
            for f in range(1, FAVG):
                total = jnp.where(of == f, beams[f * BEAMS : (f + 1) * BEAMS], total)
            first = pl.multiple_of(((chunk * some + o) * 2 + p) * BEAMS, BEAMS)
            sums[pl.ds(first, BEAMS), :] = total

    @pl.when(chunk == pl.num_programs(0) - 1)
    def _():
        turn_beams(sums, 2 * BEAMS, beam_ref)


def turn_beams(sums, pitch, beam_ref):
    lanes = beam_ref.shape[3]
    count = lanes // FAVG
    column = lax.broadcasted_iota(jnp.int32, (count, lanes), 1)
    spread = jnp.where(column // FAVG == lax.broadcasted_iota(jnp.int32, (count, lanes), 0), 1.0, 0.0)
    spread = spread.astype(BF16)
    fine = lax.broadcasted_iota(jnp.int32, (1, lanes), 1) % FAVG
    for p in range(2):
        for b in range(BEAMS):
            rows = sums[pl.ds(p * BEAMS + b, count, stride=pitch), :].astype(BF16)
            moved = lax.dot_general(rows, spread, TN, preferred_element_type=F32)
            for q in range(2):
                total = moved[q * 64 : q * 64 + SPEC]
                for f in range(1, FAVG):
                    total = jnp.where(fine == f, moved[q * 64 + f * SPEC : q * 64 + (f + 1) * SPEC], total)
                beam_ref[b, p, q * SPEC : (q + 1) * SPEC, :] = total.astype(BF16)


def correlate(turned, real, imag, block_pairs):
    per_dest = turned.shape[0]
    lanes = FAVG * per_dest
    some = math.gcd(per_dest, 4)
    weight_spec = pl.BlockSpec((some, FAVG * BEAMS, STATIONS), lambda o, pairs: (o, 0, 0))
    visibilities, beams = pl.pallas_call(
        correlate_kernel,
        grid_spec=pltpu.PrefetchScalarGridSpec(
            num_scalar_prefetch=1,
            grid=(per_dest // some,),
            in_specs=[
                pl.BlockSpec((some, INPUTS, R2), lambda o, pairs: (o, 0, 0)),
                weight_spec,
                weight_spec,
            ],
            out_specs=[
                pl.BlockSpec((some, PAIRS, BLK, 2 * BLK), lambda o, pairs: (o, 0, 0, 0)),
                pl.BlockSpec((BEAMS, 2, 2 * SPEC, lanes), lambda o, pairs: (0, 0, 0, 0)),
            ],
            scratch_shapes=[
                pltpu.VMEM((some, NBLK, 2 * BLK, R2), BF16),
                pltpu.VMEM((some, INPUTS, R2), F32),
                pltpu.VMEM((per_dest * 2 * BEAMS, R2), F32),
            ],
        ),
        out_shape=[
            jax.ShapeDtypeStruct((per_dest, PAIRS, BLK, 2 * BLK), BF16),
            jax.ShapeDtypeStruct((BEAMS, 2, 2 * SPEC, lanes), BF16),
        ],
        name="correlate",
    )(block_pairs.T, turned, real, imag)
    return visibilities, jnp.swapaxes(beams, 2, 3)


def beam_weights(stations, gains, delays, chan_start, per_dest):
    named = stations[:, :, None] == jnp.arange(STATIONS, dtype=jnp.int32)[None, None, :]
    gain = jnp.sum(jnp.where(named, gains[:, :, None] / math.sqrt(LIST), 0.0), axis=1)
    delay = jnp.sum(jnp.where(named, delays[:, :, None], 0.0), axis=1)
    rate = 2.0 * math.pi / NFFT * delay
    coarse = (chan_start + FAVG * jnp.arange(per_dest, dtype=jnp.int32)).astype(F32)
    base = rate[None] * coarse[:, None, None]
    base_cos, base_sin = gain * jnp.cos(base), gain * jnp.sin(base)
    fine = rate[None] * jnp.arange(FAVG, dtype=jnp.int32).astype(F32)[:, None, None]
    fine_cos, fine_sin = jnp.cos(fine)[None], jnp.sin(fine)[None]
    base_cos, base_sin = base_cos[:, None], base_sin[:, None]
    real = base_cos * fine_cos - base_sin * fine_sin
    imag = -(base_sin * fine_cos + base_cos * fine_sin)
    shape = (per_dest, FAVG * BEAMS, STATIONS)
    return real.astype(BF16).reshape(shape), imag.astype(BF16).reshape(shape)


def shards(voltages, filter_taps, beam_stations, beam_gain, beam_delay, block_pairs):
    stn = lax.axis_size("stn")
    chan = lax.axis_size("chan")
    devices = stn * chan
    per_dest = OUTCH // devices
    chan_start = (lax.axis_index("stn") * chan + lax.axis_index("chan")) * (NFFT // devices)
    if voltages.shape[0] % SEND_GROUP == 0 and voltages.shape[0] > LATE and per_dest % GROUPS == 0:
        return fused(
            voltages, filter_taps, beam_stations, beam_gain, beam_delay, block_pairs, stn, chan
        )
    turned, gains, delays = spectra_of_channels(
        voltages, filter_taps, beam_gain, beam_delay, stn, chan
    )
    real, imag = beam_weights(beam_stations, gains, delays, chan_start, per_dest)
    return correlate(turned, real, imag, block_pairs)


def solution(mesh):
    placed = (P(("stn", "chan"), None, None, None), P(), P(), P("stn", None), P("stn", None), P())
    return jax.shard_map(
        shards,
        mesh=mesh,
        in_specs=placed,
        out_specs=(P(("stn", "chan"), None, None, None), P(None, None, ("stn", "chan"), None)),
        check_vma=False,
    )
```

```python
import functools
import math

import jax
import jax.numpy as jnp
import numpy as np
from jax import lax
from jax.experimental import pallas as pl
from jax.experimental.pallas import tpu as pltpu
from jax.sharding import PartitionSpec as P

STATIONS = 512
INPUTS = 1024
NFFT = 4096
BEAMS = 16
TAPS = 12
FAVG = 4
BLK = 64
LIST = 128
SPEC = 16
FRAMES = 27
NBLK = 16
PAIRS = 16
R1 = 32
R2 = 128
GROUPS = R1 // FAVG
OUTCH = NFFT // FAVG
SEND_GROUP = 2
LATE = 20
CHUNK = 2
ROWS = 40
PITCH = 24
SUMS = 40
F32 = jnp.float32
BF16 = jnp.bfloat16
NT = (((1,), (1,)), ((), ()))
TN = (((0,), (0,)), ((), ()))


def tables():
    b = np.arange(R2)
    ang = 2.0 * np.pi * (b[:, None] * b[None, :] % R2) / R2
    f2 = np.block([[np.cos(ang), np.sin(ang)], [-np.sin(ang), np.cos(ang)]])
    hi = f2.astype(jnp.bfloat16)
    lo = (f2 - hi.astype(np.float64)).astype(jnp.bfloat16)
    f2 = np.concatenate([hi, lo], axis=0)
    ang = 2.0 * np.pi * (np.arange(R1)[:, None] * b[None, :]) / NFFT
    tw = np.stack([np.cos(ang), -np.sin(ang)], axis=1) / math.sqrt(NFFT)
    ang = 2.0 * np.pi * (np.arange(8)[:, None] * np.arange(4)[None, :]) / R1
    mid = np.stack([np.cos(ang), -np.sin(ang)], axis=-1).reshape(8, 8, 1)
    mid = np.broadcast_to(mid, (8, 8, R2))
    return f2, tw.astype(np.float32), mid.astype(np.float32)


def add(x, y):
    return (x[0] + y[0], x[1] + y[1])


def sub(x, y):
    return (x[0] - y[0], x[1] - y[1])


def turn(x):
    return (x[1], -x[0])


def dft4(x):
    p, m = add(x[0], x[2]), sub(x[0], x[2])
    q, n = add(x[1], x[3]), turn(sub(x[1], x[3]))
    return [add(p, q), add(m, n), sub(p, q), sub(m, n)]


def dft8(x):
    even = dft4(x[0::2])
    odd = dft4(x[1::2])
    h = math.sqrt(0.5)
    o1, o3 = odd[1], odd[3]
    odd = [
        odd[0],
        ((o1[0] + o1[1]) * h, (o1[1] - o1[0]) * h),
        turn(odd[2]),
        ((o3[1] - o3[0]) * h, -(o3[0] + o3[1]) * h),
    ]
    return [add(e, o) for e, o in zip(even, odd)] + [sub(e, o) for e, o in zip(even, odd)]


def transform(group, pitch, step, v_ref, taps_ref, tw_ref, mtw_ref, f2_ref, vs, mid, y_hi, y_lo, os):
    rows = vs.reshape(2 * R1 * ROWS, R2)
    for frame in range(FRAMES):
        rows[pl.ds(frame, 2 * R1, stride=ROWS), :] = v_ref[frame].astype(F32)

    def low(a_lo, carry):
        x = []
        for a_hi in range(4):
            a = a_lo + 8 * a_hi
            parts = [None, None]
            for t in range(TAPS):
                tap = taps_ref[t : t + 1, pl.ds(pl.multiple_of(a * R2, R2), R2)]
                for q in range(2):
                    term = tap * vs[2 * a + q, t : t + SPEC, :]
                    parts[q] = term if t == 0 else parts[q] + term
            x.append(tuple(parts))
        z = dft4(x)
        for k in range(4):
            zr, zi = z[k]
            if k:
                wr = mtw_ref[a_lo, 2 * k : 2 * k + 1, :]
                wi = mtw_ref[a_lo, 2 * k + 1 : 2 * k + 2, :]
                zr, zi = zr * wr - zi * wi, zr * wi + zi * wr
            mid[k, 2 * a_lo] = zr
            mid[k, 2 * a_lo + 1] = zi
        return carry

    lax.fori_loop(0, 8, low, 0, unroll=4)
    for k in range(4):
        z = dft8([(mid[k, 2 * a], mid[k, 2 * a + 1]) for a in range(8)])
        for k2 in range(8):
            c1 = k + 4 * k2
            zr, zi = z[k2]
            wr, wi = tw_ref[c1, 0:1, :], tw_ref[c1, 1:2, :]
            for q, val in enumerate((zr * wr - zi * wi, zr * wi + zi * wr)):
                hi = val.astype(BF16)
                y_hi[c1 * SPEC : (c1 + 1) * SPEC, q * R2 : (q + 1) * R2] = hi
                y_lo[c1 * SPEC : (c1 + 1) * SPEC, q * R2 : (q + 1) * R2] = (
                    val - hi.astype(F32)
                ).astype(BF16)
    left = lax.broadcasted_iota(jnp.int32, (R2, R2), 1) < 64
    for h in range(2):
        yh = y_hi[h * 256 : (h + 1) * 256, :]
        yl = y_lo[h * 256 : (h + 1) * 256, :]
        full = lax.dot_general(f2_ref[...], yh, NT, preferred_element_type=F32)
        res = full[0:256] + full[256:512]
        res = res + lax.dot_general(f2_ref[0:256, :], yl, NT, preferred_element_type=F32)
        for j in range(2):
            re = res[0:R2, j * R2 : (j + 1) * R2]
            im = res[R2 : 2 * R2, j * R2 : (j + 1) * R2]
            first = jnp.where(left, re, pltpu.roll(im, 64, 1))
            second = jnp.where(left, pltpu.roll(re, 64, 1), im)
            g = 4 * h + 2 * j
            os[pl.ds(g * group + step, R2, stride=pitch), :] = first
            os[pl.ds((g + 1) * group + step, R2, stride=pitch), :] = second


def fft_kernel(group, v_ref, taps_ref, tw_ref, mtw_ref, f2_ref, out_ref, vs, mid, y_hi, y_lo, os):
    step = pl.program_id(1)
    transform(group, GROUPS * group, step, v_ref, taps_ref, tw_ref, mtw_ref, f2_ref, vs, mid, y_hi, y_lo, os)

    @pl.when(step == group - 1)
    def _():
        n_dest, per_dest = out_ref.shape[0], out_ref.shape[1]

        def emit(dest, carry):
            size = per_dest * group
            part = os[pl.ds(pl.multiple_of(dest * size, size), size), :]
            out_ref[dest] = part.reshape(per_dest, group, R2).astype(BF16)
            return carry

        lax.fori_loop(0, n_dest, emit, 0)


def by_sample(voltages):
    count = voltages.shape[0]
    split = voltages.reshape(count, FRAMES, 2, R1, R2)
    return jnp.transpose(split, (0, 1, 3, 2, 4)).reshape(count, FRAMES, 2 * R1, R2)


def channelize(voltages, filter_taps, devices):
    count = voltages.shape[0]
    group = min(16, count)
    per_dest = OUTCH // devices
    f2, tw, mtw = tables()
    return pl.pallas_call(
        functools.partial(fft_kernel, group),
        grid=(count // group, group),
        out_shape=jax.ShapeDtypeStruct((devices, per_dest, count, R2), BF16),
        in_specs=[
            pl.BlockSpec((None, FRAMES, 2 * R1, R2), lambda i, j: (i * group + j, 0, 0, 0)),
            pl.BlockSpec((TAPS, NFFT), lambda i, j: (0, 0)),
            pl.BlockSpec((R1, 2, R2), lambda i, j: (0, 0, 0)),
            pl.BlockSpec((8, 8, R2), lambda i, j: (0, 0, 0)),
            pl.BlockSpec((512, 256), lambda i, j: (0, 0)),
        ],
        out_specs=pl.BlockSpec((devices, per_dest, group, R2), lambda i, j: (0, 0, i, 0)),
        scratch_shapes=[
            pltpu.VMEM((2 * R1, ROWS, R2), F32),
            pltpu.VMEM((4, 16, SPEC, R2), F32),
            pltpu.VMEM((512, 256), BF16),
            pltpu.VMEM((512, 256), BF16),
            pltpu.VMEM((OUTCH * group, R2), F32),
        ],
        compiler_params=pltpu.CompilerParams(vmem_limit_bytes=48 << 20),
        name="channelize",
    )(
        by_sample(voltages),
        filter_taps,
        jnp.asarray(tw),
        jnp.asarray(mtw),
        jnp.asarray(f2),
    )


def steer(first_channel, stations, gains, delays, wr, wi):
    highest = lax.Precision.HIGHEST
    table = jnp.concatenate([gains / math.sqrt(LIST), delays * (2.0 * math.pi / NFFT)], axis=0)
    beam = lax.broadcasted_iota(jnp.int32, (2 * BEAMS, 1), 0) % BEAMS
    spread = jnp.zeros((2 * BEAMS, STATIONS), F32)
    for b in range(BEAMS):
        named = lax.broadcasted_iota(jnp.int32, (STATIONS, LIST), 0) == stations[b : b + 1, :]
        row = jnp.where(beam == b, table, 0.0)
        spread += lax.dot_general(
            row, named.astype(F32), NT, precision=highest, preferred_element_type=F32
        )
    gain, rate = spread[0:BEAMS], spread[BEAMS:]
    fine = [(jnp.cos(rate * float(f)), jnp.sin(rate * float(f))) for f in range(FAVG)]

    def one(o, carry):
        base = rate * (first_channel + FAVG * o).astype(F32)
        base_cos, base_sin = gain * jnp.cos(base), gain * jnp.sin(base)
        for f, (fine_cos, fine_sin) in enumerate(fine):
            real = base_cos * fine_cos - base_sin * fine_sin
            imag = -(base_sin * fine_cos + base_cos * fine_sin)
            wr[o, f * BEAMS : (f + 1) * BEAMS, :] = real.astype(BF16)
            wi[o, f * BEAMS : (f + 1) * BEAMS, :] = imag.astype(BF16)
        return carry

    lax.fori_loop(0, wr.shape[0], one, 0)


def station_kernel(
    stn, chan, v_ref, taps_ref, tw_ref, mtw_ref, f2_ref, pairs, stations, gain, delay, vis, last, wr, wi, sums,
    vs, mid, y_hi, y_lo, os, stage, x, gains, delays, both, wide,
    send_sem, early_sem, late_sem, own_sem, beam_send, beam_recv, beam_own,
):
    devices = stn * chan
    row, column = lax.axis_index("stn"), lax.axis_index("chan")
    me = row * chan + column
    now = pl.program_id(0)
    per_dest, parts = stage.shape[1], stage.shape[2]
    count = parts * SEND_GROUP
    late = LATE // SEND_GROUP
    early = parts - late
    some = CHUNK
    chunks = per_dest // some
    part, step = now // SEND_GROUP, now % SEND_GROUP
    barrier = pltpu.get_barrier_semaphore()
    small = ((gain, gains), (delay, delays))

    def peer(k):
        dest = lax.rem(me + k, devices)
        return dest, (dest // chan, lax.rem(dest, chan))

    def beam_copy(which, k):
        return pltpu.make_async_remote_copy(
            src_ref=small[which][0],
            dst_ref=small[which][1].at[row],
            send_sem=beam_send.at[which, k],
            recv_sem=beam_recv.at[which, k],
            device_id=(lax.rem(row + k, stn), column),
            device_id_type=pl.DeviceIdType.MESH,
        )

    def beam_keep(which):
        return pltpu.make_async_copy(small[which][0], small[which][1].at[row], beam_own.at[which])

    def copy(k, outs, first, size, sem):
        dest, where = peer(k)
        return pltpu.make_async_remote_copy(
            src_ref=stage.at[dest, outs, pl.ds(first, size)],
            dst_ref=x.at[outs, pl.ds(me * parts + first, size)],
            send_sem=send_sem,
            recv_sem=sem,
            device_id=where,
            device_id_type=pl.DeviceIdType.MESH,
        )

    def own():
        return pltpu.make_async_copy(stage.at[me], x.at[:, pl.ds(me * parts, parts)], own_sem)

    def arrived(outs, size, sem):
        ref = x.at[outs, pl.ds(0, (devices - 1) * size)]
        pltpu.make_async_copy(ref, ref, sem).wait()

    def rows_of(out, k):
        return x[out, pl.ds(k * (BLK // SEND_GROUP), BLK // SEND_GROUP)].reshape(BLK, R2)

    def fill(dest):
        size = per_dest // GROUPS
        rows = [
            os[pl.ds(pl.multiple_of((dest * size + n) * PITCH, 8), GROUPS * SEND_GROUP), :]
            for n in range(size)
        ]
        for n in range(size):
            some_rows = rows[n].reshape(GROUPS, 1, SEND_GROUP, R2).astype(BF16)
            stage[dest, n * GROUPS : (n + 1) * GROUPS, pl.ds(part, 1)] = some_rows

    @pl.when(now == 0)
    def _():
        def greet(k, carry):
            pl.semaphore_signal(
                barrier, inc=1, device_id=peer(k)[1], device_id_type=pl.DeviceIdType.MESH
            )
            return carry

        lax.fori_loop(1, devices, greet, 0)

    @pl.when(now < count)
    def _():
        transform(SEND_GROUP, PITCH, step, v_ref, taps_ref, tw_ref, mtw_ref, f2_ref, vs, mid, y_hi, y_lo, os)

    @pl.when(now == SEND_GROUP - 1)
    def _():
        pl.semaphore_wait(barrier, devices - 1)
        for which in range(2):
            for k in range(1, stn):
                beam_copy(which, k).start()
            beam_keep(which).start()

    @pl.when((now < count) & (step == SEND_GROUP - 1) & (part < early))
    def _():
        def emit(k, carry):
            fill(peer(k)[0])
            copy(k, slice(None), part, 1, early_sem).start()
            return carry

        lax.fori_loop(1, devices, emit, 0)
        fill(me)

    @pl.when((now < count) & (step == SEND_GROUP - 1) & (part >= early))
    def _():
        def emit(dest, carry):
            fill(dest)
            return carry

        lax.fori_loop(0, devices, emit, 0)

    @pl.when(now == count - 1)
    def _():
        def emit(n, carry):
            chunk, k = n // (devices - 1), 1 + lax.rem(n, devices - 1)
            copy(k, pl.ds(chunk * some, some), early, late, late_sem.at[chunk]).start()
            return carry

        lax.fori_loop(0, chunks * (devices - 1), emit, 0)
        own().start()
        for which in range(2):
            for k in range(1, stn):
                beam_copy(which, k).wait()
            beam_keep(which).wait()
        every = [jnp.concatenate([ref[r] for r in range(stn)], axis=0) for ref in (gains, delays)]
        steer(me * (per_dest * FAVG), stations[...], every[0], every[1], wr, wi)
        own().wait()
        arrived(slice(None), early, early_sem)

    @pl.when(now >= count)
    def _():
        chunk = now - count
        arrived(pl.ds(chunk * some, some), late, late_sem.at[chunk])

        @pl.when(chunk < chunks - 1)
        def _():
            correlate_chunk(chunk, chunk, pairs, rows_of, wr, wi, vis, both, wide, sums)

    @pl.when(now == count + chunks - 1)
    def _():
        def keep(n, carry):
            o, k = n // NBLK, lax.rem(n, NBLK)
            last[o, pl.ds(pl.multiple_of(k * BLK, BLK), BLK), :] = rows_of((chunks - 1) * some + o, k)
            return carry

        lax.fori_loop(0, some * NBLK, keep, 0)
        sent = stage.at[pl.ds(0, devices - 1)]
        pltpu.make_async_copy(sent, sent, send_sem).wait()


def correlate_chunk(chunk, slot, pairs, rows_of, wr_ref, wi_ref, vis_ref, both, wide, sums):
    some = CHUNK
    lane = lax.broadcasted_iota(jnp.int32, (1, R2), 1)
    sign = jnp.where(lane < 64, -1.0, 1.0).astype(F32)
    of = (lane // SPEC) % FAVG

    def one(o, carry):
        out = chunk * some + o
        for k in range(NBLK):
            x = rows_of(out, k)
            xf = x.astype(F32)
            wide[o, k * BLK : (k + 1) * BLK, :] = xf
            both[o, k, 0:BLK, :] = x
            both[o, k, BLK : 2 * BLK, :] = (pltpu.roll(xf, 64, 1) * sign).astype(BF16)
        for r in range(PAIRS):
            rows = both[o, pairs[0, r], 0:BLK, :]
            vis = lax.dot_general(rows, both[o, pairs[1, r]], NT, preferred_element_type=F32)
            vis_ref[slot * some + o, r] = (vis * (1.0 / (FAVG * SPEC))).astype(BF16)
        for p in range(2):
            x = wide.at[o][pl.ds(p, STATIONS, stride=2), :].astype(BF16)
            real = jnp.dot(wr_ref[out], x, preferred_element_type=F32)
            imag = jnp.dot(wi_ref[out], x, preferred_element_type=F32)
            beams = real + sign * pltpu.roll(imag, 64, 1)
            total = beams[0:BEAMS]
            for f in range(1, FAVG):
                total = jnp.where(of == f, beams[f * BEAMS : (f + 1) * BEAMS], total)
            first = pl.multiple_of(out * SUMS + p * BEAMS, 8)
            sums[pl.ds(first, BEAMS), :] = total
        return carry

    lax.fori_loop(0, some, one, 0)


def finish_kernel(
    pairs_ref, part_ref, x_ref, wr_ref, wi_ref, sums_ref, vis_ref, beam_ref,
    pairs, last, both, wide, sums, beams, pairs_sem, sem, beam_sem,
):
    some = CHUNK
    first = vis_ref.shape[0] - some
    held = first * SUMS

    def rows_of(out, k):
        return x_ref[out - first, k * BLK : (k + 1) * BLK, :]

    roster = pltpu.make_async_copy(pairs_ref, pairs, pairs_sem)
    roster.start()
    copies = [
        pltpu.make_async_copy(part_ref.at[pl.ds(0, first)], vis_ref.at[pl.ds(0, first)], sem.at[0]),
        pltpu.make_async_copy(last, vis_ref.at[pl.ds(first, some)], sem.at[1]),
        pltpu.make_async_copy(beams, beam_ref, beam_sem),
    ]
    copies[0].start()
    sums[0:held, :] = sums_ref[0:held, :]
    roster.wait()
    correlate_chunk(first // some, 0, pairs, rows_of, wr_ref, wi_ref, last, both, wide, sums)
    copies[1].start()
    turn_beams(sums, SUMS, beams)
    copies[2].start()
    for copy in copies:
        copy.wait()


def fused(voltages, filter_taps, stations, gain, delay, block_pairs, stn, chan):
    count = voltages.shape[0]
    devices = stn * chan
    per_dest = OUTCH // devices
    parts = count // SEND_GROUP
    some = CHUNK
    chunks = per_dest // some
    lanes = FAVG * per_dest
    f2, tw, mtw = tables()
    held = [
        pltpu.VMEM((per_dest, PAIRS, BLK, 2 * BLK), BF16),
        pltpu.VMEM((some, INPUTS, R2), BF16),
        pltpu.VMEM((per_dest, FAVG * BEAMS, STATIONS), BF16),
        pltpu.VMEM((per_dest, FAVG * BEAMS, STATIONS), BF16),
        pltpu.VMEM((per_dest * SUMS, R2), F32),
    ]
    worked = pl.pallas_call(
        functools.partial(station_kernel, stn, chan),
        grid=(count + chunks,),
        out_shape=held,
        in_specs=[
            pl.BlockSpec((None, FRAMES, 2 * R1, R2), lambda i: (jnp.minimum(i, count - 1), 0, 0, 0)),
            pl.BlockSpec((TAPS, NFFT), lambda i: (0, 0)),
            pl.BlockSpec((R1, 2, R2), lambda i: (0, 0, 0)),
            pl.BlockSpec((8, 8, R2), lambda i: (0, 0, 0)),
            pl.BlockSpec((512, 256), lambda i: (0, 0)),
            pl.BlockSpec(memory_space=pltpu.SMEM),
            pl.BlockSpec((BEAMS, LIST), lambda i: (0, 0)),
            pl.BlockSpec(memory_space=pl.ANY),
            pl.BlockSpec(memory_space=pl.ANY),
        ],
        out_specs=[pl.BlockSpec(memory_space=pltpu.VMEM)] * len(held),
        scratch_shapes=[
            pltpu.VMEM((2 * R1, ROWS, R2), F32),
            pltpu.VMEM((4, 16, SPEC, R2), F32),
            pltpu.VMEM((512, 256), BF16),
            pltpu.VMEM((512, 256), BF16),
            pltpu.VMEM((R2 * PITCH, R2), F32),
            pltpu.VMEM((devices, per_dest, parts, SEND_GROUP, R2), BF16),
            pltpu.VMEM((per_dest, devices * parts, SEND_GROUP, R2), BF16),
            pltpu.VMEM((stn,) + gain.shape, F32),
            pltpu.VMEM((stn,) + delay.shape, F32),
            pltpu.VMEM((some, NBLK, 2 * BLK, R2), BF16),
            pltpu.VMEM((some, INPUTS, R2), F32),
            pltpu.SemaphoreType.DMA,
            pltpu.SemaphoreType.DMA,
            pltpu.SemaphoreType.DMA((chunks,)),
            pltpu.SemaphoreType.DMA,
            pltpu.SemaphoreType.DMA((2, stn)),
            pltpu.SemaphoreType.DMA((2, stn)),
            pltpu.SemaphoreType.DMA((2,)),
        ],
        compiler_params=pltpu.CompilerParams(
            vmem_limit_bytes=48 << 20, collective_id=0, has_side_effects=True
        ),
        name="station_beamformer",
    )(
        by_sample(voltages),
        filter_taps,
        jnp.asarray(tw),
        jnp.asarray(mtw),
        jnp.asarray(f2),
        block_pairs.T,
        stations,
        gain,
        delay,
    )
    whole = pl.BlockSpec(memory_space=pltpu.VMEM)
    visibilities, beams = pl.pallas_call(
        finish_kernel,
        out_shape=[
            jax.ShapeDtypeStruct((per_dest, PAIRS, BLK, 2 * BLK), BF16),
            jax.ShapeDtypeStruct((BEAMS, 2, 2 * SPEC, lanes), BF16),
        ],
        in_specs=[pl.BlockSpec(memory_space=pl.ANY)] + [whole] * len(held),
        out_specs=[pl.BlockSpec(memory_space=pl.ANY)] * 2,
        scratch_shapes=[
            pltpu.SMEM((2, PAIRS), jnp.int32),
            pltpu.VMEM((some, PAIRS, BLK, 2 * BLK), BF16),
            pltpu.VMEM((some, NBLK, 2 * BLK, R2), BF16),
            pltpu.VMEM((some, INPUTS, R2), F32),
            pltpu.VMEM((per_dest * SUMS, R2), F32),
            pltpu.VMEM((BEAMS, 2, 2 * SPEC, lanes), BF16),
            pltpu.SemaphoreType.DMA,
            pltpu.SemaphoreType.DMA((2,)),
            pltpu.SemaphoreType.DMA,
        ],
        compiler_params=pltpu.CompilerParams(vmem_limit_bytes=16 << 20),
        name="finish",
    )(block_pairs.T, *worked)
    return visibilities, jnp.swapaxes(beams, 2, 3)


def spectra_of_channels(voltages, filter_taps, gain, delay, stn, chan):
    count = voltages.shape[0]
    devices = stn * chan
    per_dest = OUTCH // devices
    spectra = channelize(voltages, filter_taps, devices)
    moved = lax.all_to_all(spectra, ("stn", "chan"), split_axis=0, concat_axis=0, tiled=True)
    turned = jnp.transpose(moved, (1, 0, 2, 3)).reshape(per_dest, devices * count, R2)
    gains = lax.all_gather(gain, "stn", axis=0, tiled=True)
    delays = lax.all_gather(delay, "stn", axis=0, tiled=True)
    return turned, gains, delays


def correlate_kernel(pairs, x_ref, wr_ref, wi_ref, vis_ref, beam_ref, both, wide, sums):
    chunk = pl.program_id(0)
    some = x_ref.shape[0]
    lane = lax.broadcasted_iota(jnp.int32, (1, R2), 1)
    sign = jnp.where(lane < 64, -1.0, 1.0).astype(F32)
    of = (lane // SPEC) % FAVG
    for o in range(some):
        for k in range(NBLK):
            x = x_ref[o, k * BLK : (k + 1) * BLK, :]
            xf = x.astype(F32)
            wide[o, k * BLK : (k + 1) * BLK, :] = xf
            both[o, k, 0:BLK, :] = x
            both[o, k, BLK : 2 * BLK, :] = (pltpu.roll(xf, 64, 1) * sign).astype(BF16)
        for r in range(PAIRS):
            rows = both[o, pairs[0, r], 0:BLK, :]
            vis = lax.dot_general(rows, both[o, pairs[1, r]], NT, preferred_element_type=F32)
            vis_ref[o, r] = (vis * (1.0 / (FAVG * SPEC))).astype(BF16)
        for p in range(2):
            x = wide.at[o][pl.ds(p, STATIONS, stride=2), :].astype(BF16)
            real = jnp.dot(wr_ref[o], x, preferred_element_type=F32)
            imag = jnp.dot(wi_ref[o], x, preferred_element_type=F32)
            beams = real + sign * pltpu.roll(imag, 64, 1)
            total = beams[0:BEAMS]
            for f in range(1, FAVG):
                total = jnp.where(of == f, beams[f * BEAMS : (f + 1) * BEAMS], total)
            first = pl.multiple_of(((chunk * some + o) * 2 + p) * BEAMS, BEAMS)
            sums[pl.ds(first, BEAMS), :] = total

    @pl.when(chunk == pl.num_programs(0) - 1)
    def _():
        turn_beams(sums, 2 * BEAMS, beam_ref)


def turn_beams(sums, pitch, beam_ref):
    lanes = beam_ref.shape[3]
    count = lanes // FAVG
    column = lax.broadcasted_iota(jnp.int32, (count, lanes), 1)
    spread = jnp.where(column // FAVG == lax.broadcasted_iota(jnp.int32, (count, lanes), 0), 1.0, 0.0)
    spread = spread.astype(BF16)
    fine = lax.broadcasted_iota(jnp.int32, (1, lanes), 1) % FAVG
    for p in range(2):
        for b in range(BEAMS):
            rows = sums[pl.ds(p * BEAMS + b, count, stride=pitch), :].astype(BF16)
            moved = lax.dot_general(rows, spread, TN, preferred_element_type=F32)
            for q in range(2):
                total = moved[q * 64 : q * 64 + SPEC]
                for f in range(1, FAVG):
                    total = jnp.where(fine == f, moved[q * 64 + f * SPEC : q * 64 + (f + 1) * SPEC], total)
                beam_ref[b, p, q * SPEC : (q + 1) * SPEC, :] = total.astype(BF16)


def correlate(turned, real, imag, block_pairs):
    per_dest = turned.shape[0]
    lanes = FAVG * per_dest
    some = math.gcd(per_dest, 4)
    weight_spec = pl.BlockSpec((some, FAVG * BEAMS, STATIONS), lambda o, pairs: (o, 0, 0))
    visibilities, beams = pl.pallas_call(
        correlate_kernel,
        grid_spec=pltpu.PrefetchScalarGridSpec(
            num_scalar_prefetch=1,
            grid=(per_dest // some,),
            in_specs=[
                pl.BlockSpec((some, INPUTS, R2), lambda o, pairs: (o, 0, 0)),
                weight_spec,
                weight_spec,
            ],
            out_specs=[
                pl.BlockSpec((some, PAIRS, BLK, 2 * BLK), lambda o, pairs: (o, 0, 0, 0)),
                pl.BlockSpec((BEAMS, 2, 2 * SPEC, lanes), lambda o, pairs: (0, 0, 0, 0)),
            ],
            scratch_shapes=[
                pltpu.VMEM((some, NBLK, 2 * BLK, R2), BF16),
                pltpu.VMEM((some, INPUTS, R2), F32),
                pltpu.VMEM((per_dest * 2 * BEAMS, R2), F32),
            ],
        ),
        out_shape=[
            jax.ShapeDtypeStruct((per_dest, PAIRS, BLK, 2 * BLK), BF16),
            jax.ShapeDtypeStruct((BEAMS, 2, 2 * SPEC, lanes), BF16),
        ],
        name="correlate",
    )(block_pairs.T, turned, real, imag)
    return visibilities, jnp.swapaxes(beams, 2, 3)


def beam_weights(stations, gains, delays, chan_start, per_dest):
    named = stations[:, :, None] == jnp.arange(STATIONS, dtype=jnp.int32)[None, None, :]
    gain = jnp.sum(jnp.where(named, gains[:, :, None] / math.sqrt(LIST), 0.0), axis=1)
    delay = jnp.sum(jnp.where(named, delays[:, :, None], 0.0), axis=1)
    rate = 2.0 * math.pi / NFFT * delay
    coarse = (chan_start + FAVG * jnp.arange(per_dest, dtype=jnp.int32)).astype(F32)
    base = rate[None] * coarse[:, None, None]
    base_cos, base_sin = gain * jnp.cos(base), gain * jnp.sin(base)
    fine = rate[None] * jnp.arange(FAVG, dtype=jnp.int32).astype(F32)[:, None, None]
    fine_cos, fine_sin = jnp.cos(fine)[None], jnp.sin(fine)[None]
    base_cos, base_sin = base_cos[:, None], base_sin[:, None]
    real = base_cos * fine_cos - base_sin * fine_sin
    imag = -(base_sin * fine_cos + base_cos * fine_sin)
    shape = (per_dest, FAVG * BEAMS, STATIONS)
    return real.astype(BF16).reshape(shape), imag.astype(BF16).reshape(shape)


def shards(voltages, filter_taps, beam_stations, beam_gain, beam_delay, block_pairs):
    stn = lax.axis_size("stn")
    chan = lax.axis_size("chan")
    devices = stn * chan
    per_dest = OUTCH // devices
    chan_start = (lax.axis_index("stn") * chan + lax.axis_index("chan")) * (NFFT // devices)
    if voltages.shape[0] % SEND_GROUP == 0 and voltages.shape[0] > LATE and per_dest % GROUPS == 0:
        return fused(
            voltages, filter_taps, beam_stations, beam_gain, beam_delay, block_pairs, stn, chan
        )
    turned, gains, delays = spectra_of_channels(
        voltages, filter_taps, beam_gain, beam_delay, stn, chan
    )
    real, imag = beam_weights(beam_stations, gains, delays, chan_start, per_dest)
    return correlate(turned, real, imag, block_pairs)


def solution(mesh):
    placed = (P(("stn", "chan"), None, None, None), P(), P(), P("stn", None), P("stn", None), P())
    return jax.shard_map(
        shards,
        mesh=mesh,
        in_specs=placed,
        out_specs=(P(("stn", "chan"), None, None, None), P(None, None, ("stn", "chan"), None)),
        check_vma=False,
    )
```
